256 devices in a mesh: ctx: 64 (over x, z, core), head: 4 (over y).
Axes of the slice: x: 4, y: 4, z: 8, core: 2. Of those that a mesh axis runs over, the one named last changes fastest.
Arguments:
- queries: bfloat16 [16384, 2560], P('ctx', 'head'), may hold values from -130 to 130
- keys: bfloat16 [16384, 2560], P('ctx', 'head'), may hold values from -7 to 7
- values: bfloat16 [16384, 2560], P('ctx', 'head'), may hold values from -6 to 6
- out_weight: bfloat16 [2560, 5120], P('head'), may hold values from -0.125 to 0.125
- reward_grad: bfloat16 [16384, 5120], P('ctx', 'head'), may hold values from -6 to 6
- tile_mask: int32 [128, 10], replicated, may hold values from 0 to 1, as said below
Outputs:
- grad_queries: bfloat16 [16384, 2560], P('ctx', 'head')
- grad_keys: bfloat16 [16384, 2560], P('ctx', 'head')
- grad_values: bfloat16 [16384, 2560], P('ctx', 'head')
The draws below stay inside these ranges and needn't reach their ends.
Inputs may be any that keep to these rules, and one draw needn't show every extreme that they name: `tile_mask`: entries are 0 or 1. The column 4 + (row % 2), a query tile's own tile, is always 1; columns that name a tile outside the sequence are 0.
All inputs are finite; a program needn't handle non-finite values.
Results may differ from the reference program's by a relative error of at most 0.033.
Values may be sent and summed in bfloat16 or wider, within the bound.
A program may use at most 128 MiB of HBM per device.

```python
import math
import jax
import jax.numpy as jnp
from jax import lax

D = 5120
HEAD_DIM = 128
HEADS = 20
TILE = 128
SPAN = 2
TOK_DEV = 256
TOKENS = 16384
TILES_DEV = 2
TILES = 128
WIN_TILES = 10


def shared_query_key(key):
    base = jax.random.fold_in(key, 11)
    key_q, key_k = jax.random.split(base, 2)
    feat_width = HEADS * HEAD_DIM
    full_shape = (TOKENS, feat_width)
    query_draw = jnp.clip(jax.random.normal(key_q, full_shape, jnp.float32), -6.0, 6.0)
    key_draw = jnp.clip(jax.random.normal(key_k, full_shape, jnp.float32), -6.0, 6.0)
    return (query_draw, key_draw)


def draw_queries(key, part):
    return shared_query_key(key)[0].astype(jnp.bfloat16)


def draw_keys(key, part):
    return shared_query_key(key)[1].astype(jnp.bfloat16)


def draw_tile_mask(key, part):
    base = jax.random.fold_in(key, 23)
    key_level, key_tiles = jax.random.split(base, 2)
    block_count = TOKENS // TOK_DEV
    level = jax.random.randint(key_level, (block_count,), 1, 9)
    draws = jax.random.randint(key_tiles, (TILES, WIN_TILES), 0, 8)
    tile_idx = jnp.arange(TILES, dtype=jnp.int32)
    block_of = tile_idx // TILES_DEV
    local_tile = tile_idx % TILES_DEV
    column_idx = jnp.arange(WIN_TILES, dtype=jnp.int32)
    target = (block_of[:, None] - SPAN) * TILES_DEV + column_idx[None, :]
    in_range = (target >= 0) & (target < TILES)
    chosen = draws < level[block_of][:, None]
    diagonal = column_idx[None, :] == SPAN * TILES_DEV + local_tile[:, None]
    return jnp.where(diagonal, 1, jnp.where(chosen & in_range, 1, 0)).astype(jnp.int32)


def shard_levels(stream_key, dims, shards, smallest, high):
    level, own = 1.0, jax.random.fold_in(stream_key, 6)
    for axis_at, shards_of in shards:
        steps = jnp.exp(jax.random.uniform(jax.random.fold_in(own, axis_at), (shards_of,), jnp.float32, smallest / len(shards), high / len(shards)))
        level = level * jnp.repeat(steps, dims[axis_at] // shards_of).reshape([-1 if axis == axis_at else 1 for axis in range(len(dims))])
    return level


def normal_values(rng, shape, deviation, reach, cuts=(), held_as=jnp.bfloat16):
    entries = jax.random.normal(rng, shape, jnp.float32) * deviation
    if len(cuts) > 0:
        entries = shard_levels(rng, shape, cuts, -0.22, 0.18) * entries
    return jnp.clip(entries, min=-reach, max=reach).astype(held_as)


def setup_inputs(seed: int = 0) -> dict:
    splits = jax.random.split(jax.random.key(seed), 7)
    return {
        "queries": draw_queries(jax.random.fold_in(splits[6], 71), 0),
        "keys": draw_keys(jax.random.fold_in(splits[6], 71), 0),
        "values": normal_values(splits[2], (TOKENS, HEADS * HEAD_DIM), 1.0, 6.0, ((0, 64), (1, 4))),
        "out_weight": normal_values(splits[3], (HEADS * HEAD_DIM, D), (HEADS * HEAD_DIM) ** -0.5, 0.125, ((0, 4),)),
        "reward_grad": normal_values(splits[4], (TOKENS, D), 1.0, 6.0, ((0, 64), (1, 4))),
        "tile_mask": draw_tile_mask(jax.random.fold_in(splits[6], 71), 0),
    }


def rounded(array_in):
    return lax.optimization_barrier(array_in.astype(jnp.bfloat16)).astype(jnp.float32)

def attend_block(query_blk, key_win, value_win, grad_blk, live_pairs, score_scale):
    scores = jnp.einsum('qhd,khd->hqk', query_blk, key_win) * score_scale
    live_three = live_pairs[None, :, :]
    row_max = lax.optimization_barrier(jnp.max(jnp.where(live_three, scores, -jnp.inf), axis=-1, keepdims=True))
    weights = jnp.where(live_three, jnp.exp(scores - row_max), 0.0)
    totals = lax.optimization_barrier(jnp.sum(weights, axis=-1, keepdims=True))
    attn_out = rounded(jnp.einsum('hqk,khd->hqd', rounded(weights), value_win) / totals)
    grad_heads = jnp.transpose(grad_blk, (1, 0, 2))
    delta = lax.optimization_barrier(jnp.sum(grad_heads * attn_out, axis=-1, keepdims=True))
    probs = weights / totals
    grad_value_win = jnp.einsum('hqk,hqd->khd', rounded(probs), grad_heads)
    dprobs = jnp.einsum('hqd,khd->hqk', grad_heads, value_win)
    dscores = rounded(probs * (dprobs - delta))
    grad_query_blk = (jnp.einsum('hqk,khd->qhd', dscores, key_win) * score_scale).astype(jnp.bfloat16)
    grad_key_win = jnp.einsum('hqk,qhd->khd', dscores, query_blk) * score_scale
    return (grad_query_blk, grad_key_win, grad_value_win)

def reference(queries, keys, values, out_weight, reward_grad, tile_mask):
    feat_width = HEADS * HEAD_DIM
    score_scale = 1.0 / math.sqrt(HEAD_DIM)
    block_count = TOKENS // TOK_DEV
    window_len = (2 * SPAN + 1) * TOK_DEV
    margin = SPAN * TOK_DEV
    d_out = jnp.dot(reward_grad, out_weight.T, preferred_element_type=jnp.float32).astype(jnp.bfloat16)
    key_padded = jnp.pad(keys, ((margin, margin), (0, 0)))
    value_padded = jnp.pad(values, ((margin, margin), (0, 0)))
    columns = jnp.arange(WIN_TILES, dtype=jnp.int32)

    def one_block(carry, block_idx):
        grad_key_all, grad_value_all = carry
        first = (block_idx * TOK_DEV).astype(jnp.int32)
        query_blk = lax.dynamic_slice_in_dim(queries, first, TOK_DEV, 0).astype(jnp.float32).reshape(TOK_DEV, HEADS, HEAD_DIM)
        key_win = lax.dynamic_slice_in_dim(key_padded, first, window_len, 0).astype(jnp.float32).reshape(window_len, HEADS, HEAD_DIM)
        value_win = lax.dynamic_slice_in_dim(value_padded, first, window_len, 0).astype(jnp.float32).reshape(window_len, HEADS, HEAD_DIM)
        grad_blk = lax.dynamic_slice_in_dim(d_out, first, TOK_DEV, 0).astype(jnp.float32).reshape(TOK_DEV, HEADS, HEAD_DIM)
        mask_rows = lax.dynamic_slice_in_dim(tile_mask, (block_idx * TILES_DEV).astype(jnp.int32), TILES_DEV, 0)
        target = (block_idx - SPAN).astype(jnp.int32) * TILES_DEV + columns
        tile_live = (mask_rows > 0) & ((target >= 0) & (target < TILES))[None, :]
        live_pairs = jnp.broadcast_to(tile_live[:, None, :, None], (TILES_DEV, TILE, WIN_TILES, TILE)).reshape(TOK_DEV, window_len)
        grad_query_blk, grad_key_win, grad_value_win = attend_block(query_blk, key_win, value_win, grad_blk, live_pairs, score_scale)
        grad_key_all = lax.dynamic_update_slice_in_dim(grad_key_all, lax.dynamic_slice_in_dim(grad_key_all, first, window_len, 0) + grad_key_win.reshape(window_len, feat_width), first, 0)
        grad_value_all = lax.dynamic_update_slice_in_dim(grad_value_all, lax.dynamic_slice_in_dim(grad_value_all, first, window_len, 0) + grad_value_win.reshape(window_len, feat_width), first, 0)
        return ((grad_key_all, grad_value_all), grad_query_blk.reshape(TOK_DEV, feat_width))
    start_zero = jnp.zeros((TOKENS + 2 * margin, feat_width), jnp.float32)
    (grad_key_all, grad_value_all), grad_query_parts = lax.scan(one_block, (start_zero, start_zero), jnp.arange(block_count, dtype=jnp.int32))
    grad_queries = grad_query_parts.reshape(TOKENS, feat_width)
    grad_keys = grad_key_all[margin:margin + TOKENS].astype(jnp.bfloat16)
    grad_values = grad_value_all[margin:margin + TOKENS].astype(jnp.bfloat16)
    return (grad_queries, grad_keys, grad_values)
```

```python
import functools
import math

import jax
import jax.numpy as jnp
from jax import lax
from jax.experimental import pallas as pl
from jax.experimental.pallas import tpu as pltpu
from jax.sharding import PartitionSpec as P

HEAD_DIM = 128
TILE = 128
SPAN = 2
SLOTS = 2 * SPAN + 1
OWN = SPAN
ROWS = 2 * TILE
STAT_ROWS = 8
NEG = -1.0e30
LOG2E = 1.4426950408889634
MESH = pl.DeviceIdType.MESH


def dot_nt(a, b):
    return lax.dot_general(a, b, (((1,), (1,)), ((), ())), preferred_element_type=jnp.float32)


def dot_nn(a, b):
    return lax.dot_general(a, b, (((1,), (0,)), ((), ())), preferred_element_type=jnp.float32)


def kernel(
    num_ctx,
    num_head,
    q_hbm,
    k_hbm,
    v_hbm,
    w_hbm,
    g_hbm,
    mask_hbm,
    dq_ref,
    dk_ref,
    dv_ref,
    kwin,
    vwin,
    qwin,
    dwin,
    gwin,
    wv,
    mask_sm,
    acc,
    e_scr,
    pt_scr,
    o_scr,
    linv_scr,
    dcol_scr,
    comb_scr,
    lse_win,
    del_win,
    loc_sem,
    kvq_send,
    kvq_recv,
    y_send,
    y_recv,
    d_send,
    d_recv,
    st_send,
    st_recv,
):
    heads = q_hbm.shape[1] // HEAD_DIM
    feat = g_hbm.shape[1]
    pos = lax.axis_index("ctx")
    hd = lax.axis_index("head")
    par = lax.rem(pos, 2)
    scale = 1.0 / math.sqrt(HEAD_DIM)
    scale2 = scale * LOG2E

    def at_ctx(off):
        return (lax.rem(pos + (off + num_ctx), num_ctx), hd)

    def at_head(off):
        return (pos, lax.rem(hd + (off + num_head), num_head))

    sibling = (pos + 1 - 2 * par, hd)

    local = [
        pltpu.make_async_copy(g_hbm, gwin.at[0], loc_sem.at[0]),
        pltpu.make_async_copy(w_hbm, wv, loc_sem.at[1]),
        pltpu.make_async_copy(q_hbm, qwin.at[OWN], loc_sem.at[2]),
        pltpu.make_async_copy(k_hbm, kwin.at[OWN], loc_sem.at[3]),
        pltpu.make_async_copy(v_hbm, vwin.at[OWN], loc_sem.at[4]),
        pltpu.make_async_copy(mask_hbm, mask_sm, loc_sem.at[5]),
    ]
    for copy in local:
        copy.start()

    barrier = pltpu.get_barrier_semaphore()
    partners = [at_ctx(-2), at_ctx(-1), at_ctx(1), at_ctx(2), at_head(1), at_head(-1)]
    for who in partners:
        pl.semaphore_signal(barrier, inc=1, device_id=who, device_id_type=MESH)
    pl.semaphore_wait(barrier, len(partners))

    def remote(src, dst, ssem, rsem, who):
        return pltpu.make_async_remote_copy(
            src_ref=src, dst_ref=dst, send_sem=ssem, recv_sem=rsem, device_id=who, device_id_type=MESH
        )

    lo, hi = pl.ds(0, TILE), pl.ds(TILE, TILE)
    up, down = at_head(1), at_head(-1)
    y_up_lo = remote(g_hbm.at[lo], gwin.at[1, lo], y_send.at[0], y_recv.at[0], up)
    y_up_hi = remote(g_hbm.at[hi], gwin.at[1, hi], y_send.at[1], y_recv.at[1], up)
    y_dn_hi = remote(g_hbm.at[hi], gwin.at[3, hi], y_send.at[2], y_recv.at[2], down)
    y_dn_lo = remote(g_hbm.at[lo], gwin.at[3, lo], y_send.at[3], y_recv.at[3], down)
    y_fw_lo = remote(gwin.at[1, lo], gwin.at[2, lo], y_send.at[4], y_recv.at[4], up)
    y_fw_hi = remote(gwin.at[3, hi], gwin.at[2, hi], y_send.at[5], y_recv.at[5], down)

    far_slot = 2 * SPAN - 2 * SPAN * par
    relay_dst = 3 - 2 * par
    near_dst = 1 + 2 * par

    def window(src, win, ssem, rsem):
        above = remote(src, win.at[0], ssem.at[0], rsem.at[0], at_ctx(2))
        below = remote(src, win.at[4], ssem.at[1], rsem.at[4], at_ctx(-2))
        near = remote(src, win.at[near_dst], ssem.at[2], rsem.at[near_dst], sibling)
        relay = remote(win.at[far_slot], win.at[relay_dst], ssem.at[3], rsem.at[relay_dst], sibling)
        return above, below, near, relay

    k_above, k_below, k_near, k_relay = window(k_hbm, kwin, kvq_send.at[0], kvq_recv.at[0])
    v_above, v_below, v_near, v_relay = window(v_hbm, vwin, kvq_send.at[1], kvq_recv.at[1])
    q_above, q_below, q_near, q_relay = window(q_hbm, qwin, kvq_send.at[2], kvq_recv.at[2])
    for copy in (y_up_lo, y_dn_hi, k_above, k_below, y_up_hi, y_dn_lo, k_near):
        copy.start()
    for copy in (v_above, v_below, v_near, q_above, q_below, q_near):
        copy.start()

    def got(win, rsem, slot):
        remote(win.at[OWN], win.at[slot], st_send.at[0, 0], rsem.at[slot], sibling).wait_recv()

    def relay_when_far(win, rsem, relay):
        got(win, rsem, 0)
        got(win, rsem, 4)
        relay.start()

    def rest_of(win, rsem):
        got(win, rsem, 1)
        got(win, rsem, 3)

    def features(slot_off):
        src = lax.rem(hd + slot_off, num_head)
        return pl.ds(pl.multiple_of(src * feat, 128), feat)

    local[0].wait()
    local[1].wait()
    acc[...] = dot_nt(gwin[0], wv[:, features(0)])
    for copy in local[2:]:
        copy.wait()

    def live_bias(value):
        return jnp.where(value > 0, 0.0, NEG).astype(jnp.float32)

    q_bias = [[live_bias(mask_sm[2 * pos + r, col]) for col in range(2 * SLOTS)] for r in range(2)]

    relay_when_far(kwin, kvq_recv.at[0], k_relay)
    y_up_lo.wait_recv()
    y_fw_lo.start()
    y_dn_hi.wait_recv()
    y_fw_hi.start()
    rest_of(kwin, kvq_recv.at[0])

    lane = lax.broadcasted_iota(jnp.int32, (ROWS, 128), 1)
    comb_scr[...] = jnp.zeros_like(comb_scr)

    def head_cols(h):
        return pl.ds(pl.multiple_of(h * HEAD_DIM, HEAD_DIM), HEAD_DIM)

    @pl.loop(0, heads)
    def _(h):
        cols = head_cols(h)
        q_h = qwin[OWN, :, cols]
        tops = [None, None]
        for j in range(SLOTS):
            s = dot_nt(q_h, kwin[j, :, cols]) * scale2
            for r in range(2):
                for t in range(2):
                    part = s[r * TILE : (r + 1) * TILE, t * TILE : (t + 1) * TILE] + q_bias[r][2 * j + t]
                    e_scr[h, r * TILE : (r + 1) * TILE, (2 * j + t) * TILE : (2 * j + t + 1) * TILE] = part
                    tops[r] = part if tops[r] is None else jnp.maximum(tops[r], part)
        for r in range(2):
            rows = pl.ds(r * TILE, TILE)
            top = jnp.max(tops[r], axis=1, keepdims=True)
            total = None
            for col in range(2 * SLOTS):
                lanes = pl.ds(col * TILE, TILE)
                e = jnp.exp2(e_scr[h, rows, lanes] - top)
                e_scr[h, rows, lanes] = e
                total = e if total is None else total + e
            total = jnp.sum(total, axis=1, keepdims=True)
            linv_scr[h, rows, :] = jnp.broadcast_to(1.0 / total, (TILE, 128))
            lse = top + jnp.log2(total)
            comb_scr[rows, :] = jnp.where(lane[:TILE] == h, lse, comb_scr[rows, :])

    lse_win[OWN] = jnp.transpose(comb_scr[...])[:STAT_ROWS, :]

    def stats(win, which):
        return [
            remote(
                win.at[OWN],
                win.at[OWN - off],
                st_send.at[which, i],
                st_recv.at[which, OWN - off],
                at_ctx(off),
            )
            for i, off in enumerate((-2, 2, -1, 1))
        ]

    lse_copies = stats(lse_win, 0)
    for copy in lse_copies:
        copy.start()

    relay_when_far(vwin, kvq_recv.at[1], v_relay)
    y_up_hi.wait_recv()
    acc[...] += dot_nt(gwin[1], wv[:, features(num_head - 1)])
    y_dn_lo.wait_recv()
    acc[...] += dot_nt(gwin[3], wv[:, features(1)])
    rest_of(vwin, kvq_recv.at[1])

    @pl.loop(0, heads)
    def _(h):
        cols = head_cols(h)
        out = None
        for j in range(SLOTS):
            e = e_scr[h, :, j * ROWS : (j + 1) * ROWS].astype(jnp.bfloat16)
            part = dot_nn(e, vwin[j, :, cols])
            out = part if out is None else out + part
        o_scr[:, cols] = (out * linv_scr[h]).astype(jnp.bfloat16)

    relay_when_far(qwin, kvq_recv.at[2], q_relay)
    y_fw_lo.wait_recv()
    y_fw_hi.wait_recv()
    d_out = acc[...] + dot_nt(gwin[2], wv[:, features(2)])
    dwin[OWN] = d_out.astype(jnp.bfloat16)

    comb_scr[...] = jnp.zeros_like(comb_scr)

    @pl.loop(0, heads)
    def _(h):
        cols = head_cols(h)
        delta = jnp.sum(
            dwin[OWN, :, cols].astype(jnp.float32) * o_scr[:, cols].astype(jnp.float32), axis=1, keepdims=True
        )
        dcol_scr[h] = jnp.broadcast_to(delta, (ROWS, 128))
        comb_scr[...] = jnp.where(lane == h, delta, comb_scr[...])

    del_win[OWN] = jnp.transpose(comb_scr[...])[:STAT_ROWS, :]

    def d_window(h):
        cols = head_cols(h)
        own = dwin.at[OWN, :, cols]
        above = remote(own, dwin.at[0, :, cols], d_send.at[h, 0], d_recv.at[h, 0], at_ctx(2))
        below = remote(own, dwin.at[4, :, cols], d_send.at[h, 1], d_recv.at[h, 4], at_ctx(-2))
        near = remote(own, dwin.at[near_dst, :, cols], d_send.at[h, 2], d_recv.at[h, near_dst], sibling)
        relay = remote(
            dwin.at[far_slot, :, cols],
            dwin.at[relay_dst, :, cols],
            d_send.at[h, 3],
            d_recv.at[h, relay_dst],
            sibling,
        )
        return above, below, near, relay

    del_copies = stats(del_win, 1)
    for h in range(heads):
        above, below, near, _ = d_window(h)
        above.start()
        below.start()
        near.start()
        if h == 0:
            for copy in del_copies:
                copy.start()

    @pl.loop(0, heads)
    def _(h):
        cols = head_cols(h)
        d_h = dwin[OWN, :, cols]
        delta = dcol_scr[h]
        linv = linv_scr[h]
        out = None
        for j in range(SLOTS):
            dp = dot_nt(d_h, vwin[j, :, cols])
            ds = []
            for t in range(2):
                e = e_scr[h, :, (2 * j + t) * TILE : (2 * j + t + 1) * TILE]
                ds.append((e * linv * (dp[:, t * TILE : (t + 1) * TILE] - delta)).astype(jnp.bfloat16))
            part = dot_nn(jnp.concatenate(ds, axis=1), kwin[j, :, cols])
            out = part if out is None else out + part
        dq_ref[:, cols] = (out * scale).astype(jnp.bfloat16)

    rest_of(qwin, kvq_recv.at[2])
    for slot in (0, 1, 3, 4):
        got(lse_win, st_recv.at[0], slot)

    k_bias = []
    for j in range(SLOTS):
        block = lax.rem(pos + (j - SPAN + num_ctx), num_ctx)
        k_bias.append(
            [[live_bias(mask_sm[2 * block + t, r + 2 * (2 * SPAN - j)]) for r in range(2)] for t in range(2)]
        )

    @pl.loop(0, heads)
    def _(h):
        cols = head_cols(h)
        k_h = kwin[OWN, :, cols]
        for j in range(SLOTS):
            st = dot_nt(k_h, qwin[j, :, cols]) * scale2
            lse = lse_win[j, pl.ds(h, 1), :]
            for t in range(2):
                lse_t = lse[:, t * TILE : (t + 1) * TILE]
                for r in range(2):
                    part = st[r * TILE : (r + 1) * TILE, t * TILE : (t + 1) * TILE]
                    pt_scr[h, j, r * TILE : (r + 1) * TILE, t * TILE : (t + 1) * TILE] = jnp.exp2(
                        part - (lse_t - k_bias[j][t][r])
                    )

    def d_got(h, slot):
        cols = head_cols(h)
        remote(
            dwin.at[OWN, :, cols], dwin.at[slot, :, cols], st_send.at[0, 0], d_recv.at[h, slot], sibling
        ).wait_recv()

    def d_relay(h):
        d_got(h, 0)
        d_got(h, 4)
        d_window(h)[3].start()

    d_relay(0)
    for slot in (0, 1, 3, 4):
        got(del_win, st_recv.at[1], slot)

    @pl.loop(0, heads)
    def _(h):
        @pl.when(h < heads - 1)
        def _():
            d_relay(h + 1)

        d_got(h, 1)
        d_got(h, 3)
        cols = head_cols(h)
        v_h = vwin[OWN, :, cols]
        dk = None
        dv = None
        for j in range(SLOTS):
            d_j = dwin[j, :, cols]
            p = pt_scr[h, j]
            part = dot_nn(p.astype(jnp.bfloat16), d_j)
            dv = part if dv is None else dv + part
            dp = dot_nt(v_h, d_j)
            ds = (p * (dp - del_win[j, pl.ds(h, 1), :])).astype(jnp.bfloat16)
            part = dot_nn(ds, qwin[j, :, cols])
            dk = part if dk is None else dk + part
        dv_ref[:, cols] = dv.astype(jnp.bfloat16)
        dk_ref[:, cols] = (dk * scale).astype(jnp.bfloat16)

    for copy in (y_up_lo, y_up_hi, y_dn_hi, y_dn_lo, y_fw_lo, y_fw_hi):
        copy.wait_send()
    for copies in (
        (k_above, k_below, k_near, k_relay),
        (v_above, v_below, v_near, v_relay),
        (q_above, q_below, q_near, q_relay),
    ):
        for copy in copies:
            copy.wait_send()
    for copy in lse_copies + del_copies:
        copy.wait_send()

    @pl.loop(0, heads)
    def _(h):
        for copy in d_window(h):
            copy.wait_send()


def local(num_ctx, num_head, queries, keys, values, out_weight, reward_grad, tile_mask):
    rows, width = queries.shape
    feat = reward_grad.shape[1]
    heads = width // HEAD_DIM
    out = jax.ShapeDtypeStruct((rows, width), jnp.bfloat16)
    win = pltpu.VMEM((SLOTS, rows, width), jnp.bfloat16)
    stat = pltpu.VMEM((SLOTS, STAT_ROWS, rows), jnp.float32)
    col = pltpu.VMEM((heads, rows, 128), jnp.float32)
    dma = pltpu.SemaphoreType.DMA
    return pl.pallas_call(
        functools.partial(kernel, num_ctx, num_head),
        out_shape=(out, out, out),
        in_specs=[pl.BlockSpec(memory_space=pl.ANY)] * 6,
        out_specs=[pl.BlockSpec(memory_space=pltpu.VMEM)] * 3,
        scratch_shapes=[
            win,
            win,
            win,
            win,
            pltpu.VMEM((num_head, rows, feat), jnp.bfloat16),
            pltpu.VMEM(out_weight.shape, jnp.bfloat16),
            pltpu.SMEM(tile_mask.shape, jnp.int32),
            pltpu.VMEM((rows, width), jnp.float32),
            pltpu.VMEM((heads, rows, SLOTS * rows), jnp.float32),
            pltpu.VMEM((heads, SLOTS, rows, rows), jnp.float32),
            pltpu.VMEM((rows, width), jnp.bfloat16),
            col,
            col,
            pltpu.VMEM((rows, 128), jnp.float32),
            stat,
            stat,
            dma((6,)),
            dma((3, 4)),
            dma((3, SLOTS)),
            dma((6,)),
            dma((6,)),
            dma((heads, 4)),
            dma((heads, SLOTS)),
            dma((2, 4)),
            dma((2, SLOTS)),
        ],
        compiler_params=pltpu.CompilerParams(
            collective_id=0, has_side_effects=True, vmem_limit_bytes=60 * 1024 * 1024
        ),
        name="halo_attention_backward",
    )(queries, keys, values, out_weight, reward_grad, tile_mask)


def solution(mesh):
    placed = (
        P("ctx", "head"),
        P("ctx", "head"),
        P("ctx", "head"),
        P("head", None),
        P("ctx", "head"),
        P(),
    )
    return jax.shard_map(
        functools.partial(local, mesh.shape["ctx"], mesh.shape["head"]),
        mesh=mesh,
        in_specs=placed,
        out_specs=(P("ctx", "head"), P("ctx", "head"), P("ctx", "head")),
        check_vma=False,
    )
```

```python
import functools
import math

import jax
import jax.numpy as jnp
from jax import lax
from jax.experimental import pallas as pl
from jax.experimental.pallas import tpu as pltpu
from jax.sharding import PartitionSpec as P

HEAD_DIM = 128
TILE = 128
SPAN = 2
SLOTS = 2 * SPAN + 1
OWN = SPAN
ROWS = 2 * TILE
STAT_ROWS = 8
NEG = -1.0e30
LOG2E = 1.4426950408889634
VMEM_MB = 60
MESH = pl.DeviceIdType.MESH


def dot_nt(a, b):
    return lax.dot_general(a, b, (((1,), (1,)), ((), ())), preferred_element_type=jnp.float32)


def dot_nn(a, b):
    return lax.dot_general(a, b, (((1,), (0,)), ((), ())), preferred_element_type=jnp.float32)


def kernel(
    num_ctx,
    num_head,
    q_hbm,
    k_hbm,
    v_hbm,
    w_hbm,
    g_hbm,
    mask_hbm,
    dq_ref,
    dk_ref,
    dv_ref,
    kwin,
    vwin,
    qwin,
    dwin,
    gwin,
    wv,
    mask_sm,
    acc,
    e_scr,
    pt_scr,
    o_scr,
    linv_scr,
    dcol_scr,
    dk_acc,
    dv_acc,
    lse_win,
    del_win,
    loc_sem,
    kvq_send,
    kvq_recv,
    y_send,
    y_recv,
    lo_send,
    lo_recv,
    d_send,
    d_recv,
    st_send,
    st_recv,
):
    heads = q_hbm.shape[1] // HEAD_DIM
    feat = g_hbm.shape[1]
    pos = lax.axis_index("ctx")
    hd = lax.axis_index("head")
    par = lax.rem(pos, 2)
    scale = 1.0 / math.sqrt(HEAD_DIM)
    scale2 = scale * LOG2E

    def at_ctx(off):
        return (lax.rem(pos + (off + num_ctx), num_ctx), hd)

    def at_head(off):
        return (pos, lax.rem(hd + (off + num_head), num_head))

    sibling = (pos + 1 - 2 * par, hd)

    local = [
        pltpu.make_async_copy(g_hbm, gwin.at[0], loc_sem.at[0]),
        pltpu.make_async_copy(w_hbm, wv, loc_sem.at[1]),
        pltpu.make_async_copy(q_hbm, qwin.at[OWN], loc_sem.at[2]),
        pltpu.make_async_copy(k_hbm, kwin.at[OWN], loc_sem.at[3]),
        pltpu.make_async_copy(v_hbm, vwin.at[OWN], loc_sem.at[4]),
        pltpu.make_async_copy(mask_hbm, mask_sm, loc_sem.at[5]),
    ]

    barrier = pltpu.get_barrier_semaphore()
    partners = [at_ctx(-2), at_ctx(-1), at_ctx(1), at_ctx(2), at_head(1), at_head(-1)]
    for who in partners:
        pl.semaphore_signal(barrier, inc=1, device_id=who, device_id_type=MESH)
    for copy in local:
        copy.start()
    pl.semaphore_wait(barrier, len(partners))

    def remote(src, dst, ssem, rsem, who):
        return pltpu.make_async_remote_copy(
            src_ref=src, dst_ref=dst, send_sem=ssem, recv_sem=rsem, device_id=who, device_id_type=MESH
        )

    up, down = at_head(1), at_head(-1)

    def quarter(n):
        return pl.ds(n * (ROWS // 4), ROWS // 4)

    y_up = [remote(g_hbm.at[quarter(n)], gwin.at[1, quarter(n)], y_send.at[n], y_recv.at[n], up) for n in range(4)]
    y_dn = [
        remote(g_hbm.at[quarter(n)], gwin.at[3, quarter(n)], y_send.at[4 + n], y_recv.at[4 + n], down)
        for n in range(4)
    ]
    y_fw = [
        remote(
            gwin.at[3 if n % 2 else 1, quarter(n)],
            gwin.at[2, quarter(n)],
            y_send.at[8 + n],
            y_recv.at[8 + n],
            down if n % 2 else up,
        )
        for n in range(4)
    ]

    far_slot = 2 * SPAN - 2 * SPAN * par
    relay_dst = 3 - 2 * par
    near_dst = 1 + 2 * par

    def window(src, win, ssem, rsem, part=None):
        def view(ref):
            return ref if part is None else ref.at[part[0], part[1]]

        return (
            remote(src, view(win.at[0]), ssem.at[0], rsem.at[0], at_ctx(2)),
            remote(src, view(win.at[4]), ssem.at[1], rsem.at[4], at_ctx(-2)),
            remote(src, view(win.at[near_dst]), ssem.at[2], rsem.at[near_dst], sibling),
            remote(
                view(win.at[far_slot]), view(win.at[relay_dst]), ssem.at[3], rsem.at[relay_dst], sibling
            ),
        )

    k_win = window(k_hbm, kwin, kvq_send.at[0], kvq_recv.at[0])
    v_win = window(v_hbm, vwin, kvq_send.at[1], kvq_recv.at[1])
    q_win = window(q_hbm, qwin, kvq_send.at[2], kvq_recv.at[2])
    for copy in (y_up[0], y_dn[1], k_win[0], k_win[1], y_up[1], y_dn[0], k_win[2], y_up[2], y_dn[3]):
        copy.start()
    for copy in v_win[:3] + q_win[:3]:
        copy.start()

    def got(rsem, view, slot):
        remote(view(OWN), view(slot), st_send.at[0, 0], rsem.at[slot], sibling).wait_recv()

    def relay_when_far(rsem, view, relay):
        got(rsem, view, 0)
        got(rsem, view, 4)
        relay.start()

    def rest_of(rsem, view):
        got(rsem, view, 1)
        got(rsem, view, 3)

    def k_view(slot):
        return kwin.at[slot]

    def v_view(slot):
        return vwin.at[slot]

    def q_view(slot):
        return qwin.at[slot]

    def weight(slot):
        src = lax.rem(hd + (num_head - slot), num_head)
        return wv[:, pl.ds(pl.multiple_of(src * feat, 128), feat)]

    def tile_rows(t):
        return slice(t * TILE, (t + 1) * TILE)

    def cols_of(h):
        return slice(h * HEAD_DIM, (h + 1) * HEAD_DIM)

    def whole(win, h):
        return win[:, :, cols_of(h)].reshape(SLOTS * ROWS, HEAD_DIM)

    def half(win, h, t):
        return win[:, tile_rows(t), cols_of(h)].reshape(SLOTS * TILE, HEAD_DIM)

    local[0].wait()
    local[1].wait()
    acc[...] = dot_nt(gwin[0], weight(0))
    for copy in local[2:]:
        copy.wait()

    def live_bias(value):
        return jnp.where(value > 0, 0.0, NEG).astype(jnp.float32)

    q_bias = [[live_bias(mask_sm[col, 2 * pos + r]) for col in range(2 * SLOTS)] for r in range(2)]

    y_up[0].wait_recv()
    y_fw[0].start()
    y_up[3].start()
    y_dn[1].wait_recv()
    y_fw[1].start()
    y_dn[2].start()

    relay_when_far(kvq_recv.at[0], k_view, k_win[3])
    rest_of(kvq_recv.at[0], k_view)

    lane = lax.broadcasted_iota(jnp.int32, (TILE, 128), 1)

    lse_cols = [jnp.zeros((TILE, 128), jnp.float32) for _ in range(2)]
    for h in range(heads):
        q_h = qwin[OWN, :, cols_of(h)]
        s = dot_nt(q_h, whole(kwin, h))
        for r in range(2):
            rows = tile_rows(r)
            top = None
            for col in range(2 * SLOTS):
                lanes = tile_rows(col)
                part = s[rows, lanes] * scale2 + q_bias[r][col]
                e_scr[h, rows, lanes] = part
                top = part if top is None else jnp.maximum(top, part)
            top = jnp.max(top, axis=1, keepdims=True)
            total = None
            for col in range(2 * SLOTS):
                lanes = tile_rows(col)
                e = jnp.exp2(e_scr[h, rows, lanes] - top)
                e_scr[h, rows, lanes] = e
                total = e if total is None else total + e
            total = jnp.sum(total, axis=1, keepdims=True)
            linv_scr[h, rows, :] = jnp.broadcast_to(1.0 / total, (TILE, 128))
            lse_cols[r] = jnp.where(lane == h, top + jnp.log2(total), lse_cols[r])
    for r in range(2):
        lse_win[OWN, :, tile_rows(r)] = jnp.transpose(lse_cols[r])[:STAT_ROWS, :]

    def stats(win, which, t):
        def view(slot):
            return win.at[slot, :, pl.ds(t * TILE, TILE)]

        return [
            remote(view(OWN), view(OWN - off), st_send.at[which, i], st_recv.at[which, OWN - off], at_ctx(off))
            for i, off in enumerate((-2, 2, -1, 1))
        ]

    def stats_got(win, which, t):
        for slot in (0, 1, 3, 4):
            got(st_recv.at[which], lambda s: win.at[s, :, pl.ds(t * TILE, TILE)], slot)

    lse_copies = stats(lse_win, 0, 0) + stats(lse_win, 1, 1)
    for copy in lse_copies:
        copy.start()

    y_up[2].wait_recv()
    y_fw[2].start()
    y_dn[3].wait_recv()
    y_fw[3].start()

    lo, hi = tile_rows(0), tile_rows(1)
    y_up[1].wait_recv()
    y_dn[0].wait_recv()
    acc[lo] += dot_nt(gwin[1, lo], weight(1)) + dot_nt(gwin[3, lo], weight(3))

    relay_when_far(kvq_recv.at[1], v_view, v_win[3])

    y_fw[0].wait_recv()
    y_fw[1].wait_recv()
    dwin[OWN, lo] = (acc[lo] + dot_nt(gwin[2, lo], weight(2))).astype(jnp.bfloat16)
    rest_of(kvq_recv.at[1], v_view)

    for h in range(heads):
        out = dot_nn(e_scr[h].astype(jnp.bfloat16), whole(vwin, h))
        o_scr[:, cols_of(h)] = (out * linv_scr[h]).astype(jnp.bfloat16)

    lo_win = window(dwin.at[OWN, pl.ds(0, TILE)], dwin, lo_send, lo_recv, (pl.ds(0, TILE), slice(None)))
    for copy in lo_win[:3]:
        copy.start()

    def delta_of(t):
        rows = tile_rows(t)
        cols = jnp.zeros((TILE, 128), jnp.float32)
        for h in range(heads):
            delta = jnp.sum(
                dwin[OWN, rows, cols_of(h)].astype(jnp.float32) * o_scr[rows, cols_of(h)].astype(jnp.float32),
                axis=1,
                keepdims=True,
            )
            dcol_scr[h, rows] = jnp.broadcast_to(delta, (TILE, 128))
            cols = jnp.where(lane == h, delta, cols)
        del_win[OWN, :, rows] = jnp.transpose(cols)[:STAT_ROWS, :]

    def own_queries(t):
        rows = tile_rows(t)
        for h in range(heads):
            dp = dot_nt(dwin[OWN, rows, cols_of(h)], whole(vwin, h))
            delta = dcol_scr[h, rows]
            linv = linv_scr[h, rows]
            ds = [
                (e_scr[h, rows, tile_rows(col)] * linv * (dp[:, tile_rows(col)] - delta)).astype(jnp.bfloat16)
                for col in range(2 * SLOTS)
            ]
            out = dot_nn(jnp.concatenate(ds, axis=1), whole(kwin, h))
            dq_ref[rows, cols_of(h)] = (out * scale).astype(jnp.bfloat16)

    delta_of(0)
    del_copies = stats(del_win, 2, 0)
    for copy in del_copies:
        copy.start()
    own_queries(0)

    y_up[3].wait_recv()
    y_dn[2].wait_recv()
    acc[hi] += dot_nt(gwin[1, hi], weight(1)) + dot_nt(gwin[3, hi], weight(3))

    relay_when_far(kvq_recv.at[2], q_view, q_win[3])

    y_fw[2].wait_recv()
    y_fw[3].wait_recv()
    dwin[OWN, hi] = (acc[hi] + dot_nt(gwin[2, hi], weight(2))).astype(jnp.bfloat16)
    delta_of(1)
    hi_copies = stats(del_win, 3, 1)

    def hi_window(h):
        part = (pl.ds(TILE, TILE), pl.ds(h * HEAD_DIM, HEAD_DIM))
        return window(dwin.at[OWN, part[0], part[1]], dwin, d_send.at[h], d_recv.at[h], part)

    hi_win = [hi_window(h) for h in range(heads)]
    for h in range(heads):
        for copy in hi_win[h][:3]:
            copy.start()
        if h == 0:
            for copy in hi_copies:
                copy.start()
    own_queries(1)

    rest_of(kvq_recv.at[2], q_view)
    stats_got(lse_win, 0, 0)
    stats_got(lse_win, 1, 1)

    k_bias = [[None, None], [None, None]]
    for t in range(2):
        for r in range(2):
            pieces = []
            for j in range(SLOTS):
                block = lax.rem(pos + (j - SPAN + num_ctx), num_ctx)
                bias = live_bias(mask_sm[r + 2 * (2 * SPAN - j), 2 * block + t])
                pieces.append(jnp.full((1, TILE), bias, jnp.float32))
            k_bias[t][r] = jnp.concatenate(pieces, axis=1)

    def stat_row(win, h, t):
        return jnp.concatenate([win[j, h : h + 1, tile_rows(t)] for j in range(SLOTS)], axis=1)

    for h in range(heads):
        k_h = kwin[OWN, :, cols_of(h)]
        for t in range(2):
            st = dot_nt(k_h, half(qwin, h, t)) * scale2
            lse = stat_row(lse_win, h, t)
            for r in range(2):
                pt_scr[h, t, tile_rows(r)] = jnp.exp2(st[tile_rows(r)] - (lse - k_bias[t][r]))

    def own_keys(h, t):
        d_t = half(dwin, h, t)
        p = pt_scr[h, t]
        dv = dot_nn(p.astype(jnp.bfloat16), d_t)
        dp = dot_nt(vwin[OWN, :, cols_of(h)], d_t)
        ds = (p * (dp - stat_row(del_win, h, t))).astype(jnp.bfloat16)
        return dot_nn(ds, half(qwin, h, t)), dv

    def lo_view(slot):
        return dwin.at[slot, pl.ds(0, TILE)]

    relay_when_far(lo_recv, lo_view, lo_win[3])
    rest_of(lo_recv, lo_view)
    stats_got(del_win, 2, 0)
    for h in range(heads):
        dk, dv = own_keys(h, 0)
        dk_acc[:, cols_of(h)] = dk
        dv_acc[:, cols_of(h)] = dv

    def hi_view(h):
        return lambda slot: dwin.at[slot, pl.ds(TILE, TILE), pl.ds(h * HEAD_DIM, HEAD_DIM)]

    relay_when_far(d_recv.at[0], hi_view(0), hi_win[0][3])
    stats_got(del_win, 3, 1)
    for h in range(heads):
        if h < heads - 1:
            relay_when_far(d_recv.at[h + 1], hi_view(h + 1), hi_win[h + 1][3])
        rest_of(d_recv.at[h], hi_view(h))
        dk, dv = own_keys(h, 1)
        dv_ref[:, cols_of(h)] = (dv_acc[:, cols_of(h)] + dv).astype(jnp.bfloat16)
        dk_ref[:, cols_of(h)] = ((dk_acc[:, cols_of(h)] + dk) * scale).astype(jnp.bfloat16)

    for copies in [y_up, y_dn, y_fw, k_win, v_win, q_win, lo_win, lse_copies, del_copies, hi_copies] + hi_win:
        for copy in copies:
            copy.wait_send()


def write_out(a_ref, b_ref, c_ref, a_out, b_out, c_out, sems):
    copies = [
        pltpu.make_async_copy(src, dst, sems.at[i])
        for i, (src, dst) in enumerate(((a_ref, a_out), (b_ref, b_out), (c_ref, c_out)))
    ]
    for copy in copies:
        copy.start()
    for copy in copies:
        copy.wait()


def local(num_ctx, num_head, queries, keys, values, out_weight, reward_grad, tile_mask):
    rows, width = queries.shape
    feat = reward_grad.shape[1]
    heads = width // HEAD_DIM
    mask_cols = tile_mask.T
    out = jax.ShapeDtypeStruct((rows, width), jnp.bfloat16)
    win = pltpu.VMEM((SLOTS, rows, width), jnp.bfloat16)
    stat = pltpu.VMEM((SLOTS, STAT_ROWS, rows), jnp.float32)
    col = pltpu.VMEM((heads, rows, 128), jnp.float32)
    full = pltpu.VMEM((rows, width), jnp.float32)
    dma = pltpu.SemaphoreType.DMA
    grads = pl.pallas_call(
        functools.partial(kernel, num_ctx, num_head),
        out_shape=(pltpu.VMEM((rows, width), jnp.bfloat16),) * 3,
        in_specs=[pl.BlockSpec(memory_space=pltpu.HBM)] * 6,
        out_specs=[pl.BlockSpec(memory_space=pltpu.VMEM)] * 3,
        scratch_shapes=[
            win,
            win,
            win,
            win,
            pltpu.VMEM((num_head, rows, feat), jnp.bfloat16),
            pltpu.VMEM(out_weight.shape, jnp.bfloat16),
            pltpu.SMEM(mask_cols.shape, jnp.int32),
            full,
            pltpu.VMEM((heads, rows, SLOTS * rows), jnp.float32),
            pltpu.VMEM((heads, 2, rows, SLOTS * TILE), jnp.float32),
            pltpu.VMEM((rows, width), jnp.bfloat16),
            col,
            col,
            full,
            full,
            stat,
            stat,
            dma((6,)),
            dma((3, 4)),
            dma((3, SLOTS)),
            dma((12,)),
            dma((12,)),
            dma((4,)),
            dma((SLOTS,)),
            dma((heads, 4)),
            dma((heads, SLOTS)),
            dma((4, 4)),
            dma((4, SLOTS)),
        ],
        compiler_params=pltpu.CompilerParams(
            collective_id=0, has_side_effects=True, vmem_limit_bytes=VMEM_MB * 1024 * 1024
        ),
        name="halo_attention_backward",
    )(*[pltpu.with_memory_space_constraint(x, pltpu.HBM) for x in (queries, keys, values, out_weight, reward_grad, mask_cols)])
    return pl.pallas_call(
        write_out,
        out_shape=(out, out, out),
        in_specs=[pl.BlockSpec(memory_space=pltpu.VMEM)] * 3,
        out_specs=[pl.BlockSpec(memory_space=pltpu.HBM)] * 3,
        scratch_shapes=[dma((3,))],
        compiler_params=pltpu.CompilerParams(vmem_limit_bytes=262144),
        name="write_out",
    )(*grads)


def solution(mesh):
    placed = (
        P("ctx", "head"),
        P("ctx", "head"),
        P("ctx", "head"),
        P("head", None),
        P("ctx", "head"),
        P(),
    )
    return jax.shard_map(
        functools.partial(local, mesh.shape["ctx"], mesh.shape["head"]),
        mesh=mesh,
        in_specs=placed,
        out_specs=(P("ctx", "head"), P("ctx", "head"), P("ctx", "head")),
        check_vma=False,
    )
```

```python
import functools
import math

import jax
import jax.numpy as jnp
from jax import lax
from jax.experimental import pallas as pl
from jax.experimental.pallas import tpu as pltpu
from jax.sharding import PartitionSpec as P

HEAD_DIM = 128
TILE = 128
SPAN = 2
SLOTS = 2 * SPAN + 1
OWN = SPAN
ROWS = 2 * TILE
STAT_ROWS = 8
NEG = -1.0e30
LOG2E = 1.4426950408889634
VMEM_MB = 60
DIRECT = 1
MESH = pl.DeviceIdType.MESH


def dot_nt(a, b):
    return lax.dot_general(a, b, (((1,), (1,)), ((), ())), preferred_element_type=jnp.float32)


def dot_nn(a, b):
    return lax.dot_general(a, b, (((1,), (0,)), ((), ())), preferred_element_type=jnp.float32)


def kernel(
    num_ctx,
    num_head,
    q_hbm,
    k_hbm,
    v_hbm,
    w_hbm,
    g_hbm,
    mask_hbm,
    dq_ref,
    dk_ref,
    dv_ref,
    kwin,
    vwin,
    qwin,
    dwin,
    gwin,
    wv,
    mask_sm,
    acc,
    e_scr,
    pt_scr,
    o_scr,
    linv_scr,
    dcol_scr,
    dk_acc,
    dv_acc,
    lse_win,
    del_win,
    loc_sem,
    kvq_send,
    kvq_recv,
    y_send,
    y_recv,
    lo_send,
    lo_recv,
    d_send,
    d_recv,
    st_send,
    st_recv,
):
    heads = q_hbm.shape[1] // HEAD_DIM
    feat = g_hbm.shape[1]
    pos = lax.axis_index("ctx")
    hd = lax.axis_index("head")
    par = lax.rem(pos, 2)
    scale = 1.0 / math.sqrt(HEAD_DIM)
    scale2 = scale * LOG2E

    def at_ctx(off):
        return (lax.rem(pos + (off + num_ctx), num_ctx), hd)

    def at_head(off):
        return (pos, lax.rem(hd + (off + num_head), num_head))

    sibling = (pos + 1 - 2 * par, hd)

    exists = {
        off: None if off == 0 else (pos >= -off if off < 0 else pos < num_ctx - off) for off in range(-SPAN, SPAN + 1)
    }
    from_relay = jnp.where(par == 0, pos, num_ctx - 1 - pos) > 0
    relays = jnp.where(par == 0, pos + SPAN, num_ctx + 1 - pos) < num_ctx

    def run(cond, action):
        if cond is None:
            action()
        else:
            pl.when(cond)(action)

    def start(items):
        for copy, cond in items:
            run(cond, copy.start)

    local = [
        pltpu.make_async_copy(g_hbm, gwin.at[0], loc_sem.at[0]),
        pltpu.make_async_copy(w_hbm, wv, loc_sem.at[1]),
        pltpu.make_async_copy(q_hbm, qwin.at[OWN], loc_sem.at[2]),
        pltpu.make_async_copy(k_hbm, kwin.at[OWN], loc_sem.at[3]),
        pltpu.make_async_copy(v_hbm, vwin.at[OWN], loc_sem.at[4]),
        pltpu.make_async_copy(mask_hbm, mask_sm, loc_sem.at[5]),
    ]

    barrier = pltpu.get_barrier_semaphore()


    def greet(who):
        return lambda: pl.semaphore_signal(barrier, inc=1, device_id=who, device_id_type=MESH)

    arrivals = 2
    for off in (-2, 2, -1, 1):
        run(exists[off], greet(at_ctx(off)))
        arrivals = arrivals + exists[off].astype(jnp.int32)
    greet(at_head(1))()
    greet(at_head(-1))()
    for copy in local:
        copy.start()
    for off in (-2, 2, -1, 1):

        @pl.when(jnp.logical_not(exists[off]))
        def _():
            for win in (kwin, vwin, qwin, dwin, lse_win, del_win):
                win[OWN + off] = jnp.zeros(win.shape[1:], win.dtype)

    pl.semaphore_wait(barrier, arrivals)

    def remote(src, dst, ssem, rsem, who):
        return pltpu.make_async_remote_copy(
            src_ref=src, dst_ref=dst, send_sem=ssem, recv_sem=rsem, device_id=who, device_id_type=MESH
        )

    up, down = at_head(1), at_head(-1)

    def quarter(n):
        return pl.ds(n * (ROWS // 4), ROWS // 4)

    y_up = [remote(g_hbm.at[quarter(n)], gwin.at[1, quarter(n)], y_send.at[n], y_recv.at[n], up) for n in range(4)]
    y_dn = [
        remote(g_hbm.at[quarter(n)], gwin.at[3, quarter(n)], y_send.at[4 + n], y_recv.at[4 + n], down)
        for n in range(4)
    ]
    y_fw = [
        remote(
            gwin.at[3 if n % 2 else 1, quarter(n)],
            gwin.at[2, quarter(n)],
            y_send.at[8 + n],
            y_recv.at[8 + n],
            down if n % 2 else up,
        )
        for n in range(4)
    ]

    far_slot = 2 * SPAN - 2 * SPAN * par
    relay_dst = 3 - 2 * par
    near_dst = 1 + 2 * par
    early, late = (OWN, 3 - 2 * par), (0, 2 * SPAN, 1 + 2 * par)

    def window(src, win, ssem, rsem, part=None):
        def view(ref):
            return ref if part is None else ref.at[part[0], part[1]]

        relay_src, relay_to = view(win.at[far_slot]), view(win.at[relay_dst])
        return (
            (remote(src, view(win.at[0]), ssem.at[0], rsem.at[0], at_ctx(2)), exists[2]),
            (remote(src, view(win.at[4]), ssem.at[1], rsem.at[4], at_ctx(-2)), exists[-2]),
            (remote(src, view(win.at[near_dst]), ssem.at[2], rsem.at[near_dst], sibling), None),
            (remote(relay_src, relay_to, ssem.at[3], rsem.at[relay_dst], sibling), relays),
        )

    k_win = window(k_hbm, kwin, kvq_send.at[0], kvq_recv.at[0])
    v_win = window(v_hbm, vwin, kvq_send.at[1], kvq_recv.at[1])
    q_win = [
        window(
            q_hbm.at[pl.ds(t * TILE, TILE)],
            qwin,
            kvq_send.at[2 + t],
            kvq_recv.at[2 + t],
            (pl.ds(t * TILE, TILE), slice(None)),
        )
        for t in range(2)
    ]
    y_up[0].start()
    y_dn[1].start()
    start(k_win[:2])
    for copy in (y_up[1], y_dn[0], y_up[2], y_dn[3]):
        copy.start()
    start(k_win[2:3] + v_win[:3] + q_win[0][:3] + q_win[1][:3])

    def got(rsem, view, slot):
        copy = remote(view(OWN), view(slot), st_send.at[0, 0], rsem.at[slot], sibling)
        run(exists[slot - OWN], copy.wait_recv)

    def relay_when_far(rsem, view, relay):
        got(rsem, view, 0)
        got(rsem, view, 4)
        start([relay])

    def rest_of(rsem, view):
        got(rsem, view, 1)
        got(rsem, view, 3)

    def k_view(slot):
        return kwin.at[slot]

    def v_view(slot):
        return vwin.at[slot]

    def q_view(t):
        return lambda slot: qwin.at[slot, pl.ds(t * TILE, TILE)]

    def weight(slot):
        src = lax.rem(hd + (num_head - slot), num_head)
        return wv[:, pl.ds(pl.multiple_of(src * feat, 128), feat)]

    def tile_rows(t):
        return slice(t * TILE, (t + 1) * TILE)

    def cols_of(h):
        return slice(h * HEAD_DIM, (h + 1) * HEAD_DIM)

    def whole(win, h):
        return win[:, :, cols_of(h)].reshape(SLOTS * ROWS, HEAD_DIM)

    def half(win, h, t, slots):
        return jnp.concatenate([win[j, tile_rows(t), cols_of(h)] for j in slots], axis=0)

    local[0].wait()
    local[1].wait()
    acc[...] = dot_nt(gwin[0], weight(0))
    for copy in local[2:]:
        copy.wait()

    def live_bias(value, off):
        live = value > 0 if exists[off] is None else jnp.logical_and(value > 0, exists[off])
        return jnp.where(live, 0.0, NEG).astype(jnp.float32)

    q_bias = [
        [live_bias(mask_sm[col, 2 * pos + r], col // 2 - SPAN) for col in range(2 * SLOTS)] for r in range(2)
    ]

    y_up[0].wait_recv()
    y_fw[0].start()
    y_up[3].start()
    y_dn[1].wait_recv()
    y_fw[1].start()
    y_dn[2].start()

    relay_when_far(kvq_recv.at[0], k_view, k_win[3])
    rest_of(kvq_recv.at[0], k_view)

    lane = lax.broadcasted_iota(jnp.int32, (TILE, 128), 1)

    lse_cols = [jnp.zeros((TILE, 128), jnp.float32) for _ in range(2)]
    for h in range(heads):
        q_h = qwin[OWN, :, cols_of(h)]
        s = dot_nt(q_h, whole(kwin, h))
        for r in range(2):
            rows = tile_rows(r)
            top = None
            for col in range(2 * SLOTS):
                lanes = tile_rows(col)
                part = s[rows, lanes] * scale2 + q_bias[r][col]
                e_scr[h, rows, lanes] = part
                top = part if top is None else jnp.maximum(top, part)
            top = jnp.max(top, axis=1, keepdims=True)
            total = None
            for col in range(2 * SLOTS):
                lanes = tile_rows(col)
                e = jnp.exp2(e_scr[h, rows, lanes] - top)
                e_scr[h, rows, lanes] = e
                total = e if total is None else total + e
            total = jnp.sum(total, axis=1, keepdims=True)
            linv_scr[h, rows, :] = jnp.broadcast_to(1.0 / total, (TILE, 128))
            lse_cols[r] = jnp.where(lane == h, top + jnp.log2(total), lse_cols[r])
    for r in range(2):
        lse_win[OWN, :, tile_rows(r)] = jnp.transpose(lse_cols[r])[:STAT_ROWS, :]

    def stats(win, which, t):
        def view(slot):
            return win.at[slot, :, pl.ds(t * TILE, TILE)]

        return [
            (
                remote(view(OWN), view(OWN - off), st_send.at[which, i], st_recv.at[which, OWN - off], at_ctx(off)),
                exists[off],
            )
            for i, off in enumerate((-2, 2, -1, 1))
        ]

    lse_copies = stats(lse_win, 0, 0) + stats(lse_win, 1, 1)
    start(lse_copies)

    y_up[2].wait_recv()
    y_fw[2].start()
    y_dn[3].wait_recv()
    y_fw[3].start()

    lo, hi = tile_rows(0), tile_rows(1)
    y_up[1].wait_recv()
    y_dn[0].wait_recv()
    acc[lo] += dot_nt(gwin[1, lo], weight(1)) + dot_nt(gwin[3, lo], weight(3))

    relay_when_far(kvq_recv.at[1], v_view, v_win[3])

    y_fw[0].wait_recv()
    y_fw[1].wait_recv()
    dwin[OWN, lo] = (acc[lo] + dot_nt(gwin[2, lo], weight(2))).astype(jnp.bfloat16)
    rest_of(kvq_recv.at[1], v_view)

    for h in range(heads):
        out = dot_nn(e_scr[h].astype(jnp.bfloat16), whole(vwin, h))
        o_scr[:, cols_of(h)] = (out * linv_scr[h]).astype(jnp.bfloat16)

    lo_win = window(dwin.at[OWN, pl.ds(0, TILE)], dwin, lo_send, lo_recv, (pl.ds(0, TILE), slice(None)))
    start(lo_win[:3])

    def delta_of(t):
        rows = tile_rows(t)
        cols = jnp.zeros((TILE, 128), jnp.float32)
        for h in range(heads):
            delta = jnp.sum(
                dwin[OWN, rows, cols_of(h)].astype(jnp.float32) * o_scr[rows, cols_of(h)].astype(jnp.float32),
                axis=1,
                keepdims=True,
            )
            dcol_scr[h, rows] = jnp.broadcast_to(delta, (TILE, 128))
            cols = jnp.where(lane == h, delta, cols)
        del_win[OWN, :, rows] = jnp.transpose(cols)[:STAT_ROWS, :]

    def own_queries(t):
        rows = tile_rows(t)
        for h in range(heads):
            dp = dot_nt(dwin[OWN, rows, cols_of(h)], whole(vwin, h))
            delta = dcol_scr[h, rows]
            linv = linv_scr[h, rows]
            ds = [
                (e_scr[h, rows, tile_rows(col)] * linv * (dp[:, tile_rows(col)] - delta)).astype(jnp.bfloat16)
                for col in range(2 * SLOTS)
            ]
            out = dot_nn(jnp.concatenate(ds, axis=1), whole(kwin, h))
            dq_ref[rows, cols_of(h)] = (out * scale).astype(jnp.bfloat16)

    def slot_bias(j, t, r):
        block = lax.rem(pos + (j - SPAN + num_ctx), num_ctx)
        there = jnp.logical_and(pos + j >= SPAN, pos + j < num_ctx + SPAN)
        live = jnp.logical_and(mask_sm[r + 2 * (2 * SPAN - j), 2 * block + t] > 0, there)
        return jnp.full((1, TILE), jnp.where(live, 0.0, NEG), jnp.float32)

    def stat_row(win, h, t, slots):
        return jnp.concatenate([win[j, h : h + 1, tile_rows(t)] for j in slots], axis=1)

    def lanes_of(slots):
        return slice(0, 2 * TILE) if slots is early else slice(2 * TILE, SLOTS * TILE)

    def weights_t(t, slots):
        bias = [jnp.concatenate([slot_bias(j, t, r) for j in slots], axis=1) for r in range(2)]
        for h in range(heads):
            st = dot_nt(kwin[OWN, :, cols_of(h)], half(qwin, h, t, slots)) * scale2
            lse = stat_row(lse_win, h, t, slots)
            for r in range(2):
                pt_scr[h, t, tile_rows(r), lanes_of(slots)] = jnp.exp2(st[tile_rows(r)] - (lse - bias[r]))

    def own_keys(h, t, slots):
        d_t = half(dwin, h, t, slots)
        p = pt_scr[h, t, :, lanes_of(slots)]
        dv = dot_nn(p.astype(jnp.bfloat16), d_t)
        dp = dot_nt(vwin[OWN, :, cols_of(h)], d_t)
        ds = (p * (dp - stat_row(del_win, h, t, slots))).astype(jnp.bfloat16)
        return dot_nn(ds, half(qwin, h, t, slots)), dv

    def add_keys(h, t, slots, first=False):
        dk, dv = own_keys(h, t, slots)
        if first:
            dk_acc[:, cols_of(h)] = dk
            dv_acc[:, cols_of(h)] = dv
        else:
            dk_acc[:, cols_of(h)] += dk
            dv_acc[:, cols_of(h)] += dv

    def got_at(rsem, win, t, slot, cols=slice(None)):
        rows = pl.ds(t * TILE, TILE)
        remote(win.at[OWN, rows, cols], win.at[slot, rows, cols], st_send.at[0, 0], rsem.at[slot], sibling).wait_recv()

    def near_stats(win, which, t):
        lanes = pl.ds(t * TILE, TILE)
        remote(
            win.at[OWN, :, lanes],
            win.at[early[1], :, lanes],
            st_send.at[0, 0],
            st_recv.at[which, early[1]],
            sibling,
        ).wait_recv()

    def far_stats(win, which, t):
        view = lambda slot: win.at[slot, :, pl.ds(t * TILE, TILE)]
        got(st_recv.at[which], view, 0)
        got(st_recv.at[which], view, 4)
        relayed(st_recv.at[which], view)

    def relayed(rsem, view):
        copy = remote(view(OWN), view(late[2]), st_send.at[0, 0], rsem.at[late[2]], sibling)
        run(from_relay, copy.wait_recv)

    delta_of(0)
    del_copies = stats(del_win, 2, 0)
    start(del_copies)
    own_queries(0)

    got_at(kvq_recv.at[2], qwin, 0, early[1])
    got_at(kvq_recv.at[3], qwin, 1, early[1])
    near_stats(lse_win, 0, 0)
    near_stats(lse_win, 1, 1)
    weights_t(0, early)
    weights_t(1, early)
    relay_when_far(kvq_recv.at[2], q_view(0), q_win[0][3])
    y_up[3].wait_recv()
    y_dn[2].wait_recv()
    acc[hi] += dot_nt(gwin[1, hi], weight(1)) + dot_nt(gwin[3, hi], weight(3))
    got_at(lo_recv, dwin, 0, early[1])
    near_stats(del_win, 2, 0)
    for h in range(heads):
        add_keys(h, 0, early, first=True)

    relayed(kvq_recv.at[2], q_view(0))
    far_stats(lse_win, 0, 0)
    far_stats(lse_win, 1, 1)
    weights_t(0, late)
    relay_when_far(kvq_recv.at[3], q_view(1), q_win[1][3])

    y_fw[2].wait_recv()
    y_fw[3].wait_recv()
    dwin[OWN, hi] = (acc[hi] + dot_nt(gwin[2, hi], weight(2))).astype(jnp.bfloat16)
    delta_of(1)
    hi_copies = stats(del_win, 3, 1)

    def hi_part(h):
        return pl.ds(TILE, TILE), pl.ds(h * HEAD_DIM, HEAD_DIM)

    def hi_view(h):
        return lambda slot: dwin.at[slot, hi_part(h)[0], hi_part(h)[1]]

    hi_win = [window(hi_view(h)(OWN), dwin, d_send.at[h], d_recv.at[h], hi_part(h)) for h in range(heads)]
    for h in range(heads - DIRECT, heads):
        view = hi_view(h)
        straight = remote(
            view(OWN),
            view(relay_dst),
            d_send.at[h, 3],
            d_recv.at[h, relay_dst],
            (lax.rem(pos + (2 * par - 1 + num_ctx), num_ctx), hd),
        )
        hi_win[h] = hi_win[h][:3] + ((straight, from_relay),)
    start(hi_win[0][:3] + tuple(hi_copies))
    for h in range(1, heads):
        start(hi_win[h] if h >= heads - DIRECT else hi_win[h][:3])

    def hi_relay(h):
        if h < heads - DIRECT:
            relay_when_far(d_recv.at[h], hi_view(h), hi_win[h][3])

    relayed(kvq_recv.at[3], q_view(1))
    weights_t(1, late)
    own_queries(1)

    def lo_view(slot):
        return dwin.at[slot, pl.ds(0, TILE)]

    relay_when_far(lo_recv, lo_view, lo_win[3])
    near_stats(del_win, 3, 1)
    for h in range(heads):
        got_at(d_recv.at[h], dwin, 1, early[1], hi_part(h)[1])
        add_keys(h, 1, early)
    hi_relay(0)
    relayed(lo_recv, lo_view)
    far_stats(del_win, 2, 0)
    add_keys(0, 0, late)
    add_keys(1, 0, late)
    hi_relay(1)
    add_keys(2, 0, late)
    add_keys(3, 0, late)
    hi_relay(2)
    add_keys(4, 0, late)
    far_stats(del_win, 3, 1)

    def finish(h):
        if h >= heads - DIRECT:
            got(d_recv.at[h], hi_view(h), 0)
            got(d_recv.at[h], hi_view(h), 4)
        relayed(d_recv.at[h], hi_view(h))
        dk, dv = own_keys(h, 1, late)
        dv_ref[:, cols_of(h)] = (dv_acc[:, cols_of(h)] + dv).astype(jnp.bfloat16)
        dk_ref[:, cols_of(h)] = ((dk_acc[:, cols_of(h)] + dk) * scale).astype(jnp.bfloat16)

    for h in range(heads):
        if h + 3 < heads:
            hi_relay(h + 3)
        finish(h)

    for copy in y_up + y_dn + y_fw:
        copy.wait_send()
    for items in [k_win, v_win, *q_win, lo_win, lse_copies, del_copies, hi_copies, *hi_win]:
        for copy, cond in items:
            run(cond, copy.wait_send)


def write_out(a_ref, b_ref, c_ref, a_out, b_out, c_out, sems):
    copies = [
        pltpu.make_async_copy(src, dst, sems.at[i])
        for i, (src, dst) in enumerate(((a_ref, a_out), (b_ref, b_out), (c_ref, c_out)))
    ]
    for copy in copies:
        copy.start()
    for copy in copies:
        copy.wait()


def local(num_ctx, num_head, queries, keys, values, out_weight, reward_grad, tile_mask):
    rows, width = queries.shape
    feat = reward_grad.shape[1]
    heads = width // HEAD_DIM
    mask_cols = tile_mask.T
    out = jax.ShapeDtypeStruct((rows, width), jnp.bfloat16)
    win = pltpu.VMEM((SLOTS, rows, width), jnp.bfloat16)
    stat = pltpu.VMEM((SLOTS, STAT_ROWS, rows), jnp.float32)
    col = pltpu.VMEM((heads, rows, 128), jnp.float32)
    full = pltpu.VMEM((rows, width), jnp.float32)
    dma = pltpu.SemaphoreType.DMA
    grads = pl.pallas_call(
        functools.partial(kernel, num_ctx, num_head),
        out_shape=(pltpu.VMEM((rows, width), jnp.bfloat16),) * 3,
        in_specs=[pl.BlockSpec(memory_space=pltpu.HBM)] * 6,
        out_specs=[pl.BlockSpec(memory_space=pltpu.VMEM)] * 3,
        scratch_shapes=[
            win,
            win,
            win,
            win,
            pltpu.VMEM((num_head, rows, feat), jnp.bfloat16),
            pltpu.VMEM(out_weight.shape, jnp.bfloat16),
            pltpu.SMEM(mask_cols.shape, jnp.int32),
            full,
            pltpu.VMEM((heads, rows, SLOTS * rows), jnp.float32),
            pltpu.VMEM((heads, 2, rows, SLOTS * TILE), jnp.float32),
            pltpu.VMEM((rows, width), jnp.bfloat16),
            col,
            col,
            full,
            full,
            stat,
            stat,
            dma((6,)),
            dma((4, 4)),
            dma((4, SLOTS)),
            dma((12,)),
            dma((12,)),
            dma((4,)),
            dma((SLOTS,)),
            dma((heads, 4)),
            dma((heads, SLOTS)),
            dma((4, 4)),
            dma((4, SLOTS)),
        ],
        compiler_params=pltpu.CompilerParams(
            collective_id=0, has_side_effects=True, vmem_limit_bytes=VMEM_MB * 1024 * 1024
        ),
        name="halo_attention_backward",
    )(*[pltpu.with_memory_space_constraint(x, pltpu.HBM) for x in (queries, keys, values, out_weight, reward_grad, mask_cols)])
    return pl.pallas_call(
        write_out,
        out_shape=(out, out, out),
        in_specs=[pl.BlockSpec(memory_space=pltpu.VMEM)] * 3,
        out_specs=[pl.BlockSpec(memory_space=pltpu.HBM)] * 3,
        scratch_shapes=[dma((3,))],
        compiler_params=pltpu.CompilerParams(vmem_limit_bytes=262144),
        name="write_out",
    )(*grads)


def solution(mesh):
    placed = (
        P("ctx", "head"),
        P("ctx", "head"),
        P("ctx", "head"),
        P("head", None),
        P("ctx", "head"),
        P(),
    )
    return jax.shard_map(
        functools.partial(local, mesh.shape["ctx"], mesh.shape["head"]),
        mesh=mesh,
        in_specs=placed,
        out_specs=(P("ctx", "head"), P("ctx", "head"), P("ctx", "head")),
        check_vma=False,
    )
```

```python
import functools
import math

import jax
import jax.numpy as jnp
from jax import lax
from jax.experimental import pallas as pl
from jax.experimental.pallas import tpu as pltpu
from jax.sharding import PartitionSpec as P

HEAD_DIM = 128
TILE = 128
SPAN = 2
SLOTS = 2 * SPAN + 1
OWN = SPAN
ROWS = 2 * TILE
STAT_ROWS = 8
NEG = -1.0e30
LOG2E = 1.4426950408889634
VMEM_MB = 60
GROUPS = ((0, 3), (3, 5))
MESH = pl.DeviceIdType.MESH


def dot_nt(a, b):
    return lax.dot_general(a, b, (((1,), (1,)), ((), ())), preferred_element_type=jnp.float32)


def dot_nn(a, b):
    return lax.dot_general(a, b, (((1,), (0,)), ((), ())), preferred_element_type=jnp.float32)


def kernel(
    num_ctx,
    num_head,
    q_hbm,
    k_hbm,
    v_hbm,
    w_hbm,
    g_hbm,
    mask_hbm,
    dq_ref,
    dk_ref,
    dv_ref,
    kwin,
    vwin,
    qwin,
    dwin,
    gwin,
    wv,
    mask_sm,
    acc,
    e_scr,
    pt_scr,
    o_scr,
    linv_scr,
    dcol_scr,
    dk_acc,
    dv_acc,
    lse_win,
    del_win,
    loc_sem,
    kvq_send,
    kvq_recv,
    y_send,
    y_recv,
    lo_send,
    lo_recv,
    d_send,
    d_recv,
    st_send,
    st_recv,
):
    heads = q_hbm.shape[1] // HEAD_DIM
    feat = g_hbm.shape[1]
    pos = lax.axis_index("ctx")
    hd = lax.axis_index("head")
    par = lax.rem(pos, 2)
    scale = 1.0 / math.sqrt(HEAD_DIM)
    scale2 = scale * LOG2E

    def at_ctx(off):
        return (lax.rem(pos + (off + num_ctx), num_ctx), hd)

    def at_head(off):
        return (pos, lax.rem(hd + (off + num_head), num_head))

    sibling = (pos + 1 - 2 * par, hd)

    exists = {
        off: None if off == 0 else (pos >= -off if off < 0 else pos < num_ctx - off) for off in range(-SPAN, SPAN + 1)
    }
    from_relay = jnp.where(par == 0, pos, num_ctx - 1 - pos) > 0
    relays = jnp.where(par == 0, pos + SPAN, num_ctx + 1 - pos) < num_ctx

    def run(cond, action):
        if cond is None:
            action()
        else:
            pl.when(cond)(action)

    def start(items):
        for copy, cond in items:
            run(cond, copy.start)

    local = [
        pltpu.make_async_copy(g_hbm, gwin.at[0], loc_sem.at[0]),
        pltpu.make_async_copy(w_hbm, wv, loc_sem.at[1]),
        pltpu.make_async_copy(q_hbm, qwin.at[OWN], loc_sem.at[2]),
        pltpu.make_async_copy(k_hbm, kwin.at[OWN], loc_sem.at[3]),
        pltpu.make_async_copy(v_hbm, vwin.at[OWN], loc_sem.at[4]),
        pltpu.make_async_copy(mask_hbm, mask_sm, loc_sem.at[5]),
    ]

    barrier = pltpu.get_barrier_semaphore()


    def greet(who):
        return lambda: pl.semaphore_signal(barrier, inc=1, device_id=who, device_id_type=MESH)

    arrivals = 2
    for off in (-2, 2, -1, 1):
        run(exists[off], greet(at_ctx(off)))
        arrivals = arrivals + exists[off].astype(jnp.int32)
    greet(at_head(1))()
    greet(at_head(-1))()
    for copy in local:
        copy.start()
    for off in (-2, 2, -1, 1):

        @pl.when(jnp.logical_not(exists[off]))
        def _():
            for win in (kwin, vwin, qwin, dwin, lse_win, del_win):
                win[OWN + off] = jnp.zeros(win.shape[1:], win.dtype)

    pl.semaphore_wait(barrier, arrivals)

    def remote(src, dst, ssem, rsem, who):
        return pltpu.make_async_remote_copy(
            src_ref=src, dst_ref=dst, send_sem=ssem, recv_sem=rsem, device_id=who, device_id_type=MESH
        )

    up, down = at_head(1), at_head(-1)

    def quarter(n):
        return pl.ds(n * (ROWS // 4), ROWS // 4)

    y_up = [remote(g_hbm.at[quarter(n)], gwin.at[1, quarter(n)], y_send.at[n], y_recv.at[n], up) for n in range(4)]
    y_dn = [
        remote(g_hbm.at[quarter(n)], gwin.at[3, quarter(n)], y_send.at[4 + n], y_recv.at[4 + n], down)
        for n in range(4)
    ]
    y_fw = [
        remote(
            gwin.at[3 if n % 2 else 1, quarter(n)],
            gwin.at[2, quarter(n)],
            y_send.at[8 + n],
            y_recv.at[8 + n],
            down if n % 2 else up,
        )
        for n in range(4)
    ]

    far_slot = 2 * SPAN - 2 * SPAN * par
    relay_dst = 3 - 2 * par
    ahead = 4 * par - 2
    relays_back = jnp.logical_and(pos - ahead >= 0, pos - ahead < num_ctx)
    relays_on = jnp.logical_and(pos + ahead >= 0, pos + ahead < num_ctx)
    near_dst = 1 + 2 * par
    early, late = (OWN, 3 - 2 * par), (0, 2 * SPAN, 1 + 2 * par)

    def window(src, win, ssem, rsem, part=None):
        def view(ref):
            return ref if part is None else ref.at[part[0], part[1]]

        relay_src, relay_to = view(win.at[far_slot]), view(win.at[relay_dst])
        return (
            (remote(src, view(win.at[4 * (1 - par)]), ssem.at[0], rsem.at[4 * (1 - par)], at_ctx(ahead)), relays_on),
            (remote(src, view(win.at[4 * par]), ssem.at[1], rsem.at[4 * par], at_ctx(-ahead)), relays_back),
            (remote(src, view(win.at[near_dst]), ssem.at[2], rsem.at[near_dst], sibling), None),
            (remote(relay_src, relay_to, ssem.at[3], rsem.at[relay_dst], sibling), relays),
        )

    k_win = window(k_hbm, kwin, kvq_send.at[0], kvq_recv.at[0])
    v_win = window(v_hbm, vwin, kvq_send.at[1], kvq_recv.at[1])
    q_win = [
        window(
            q_hbm.at[pl.ds(t * TILE, TILE)],
            qwin,
            kvq_send.at[2 + t],
            kvq_recv.at[2 + t],
            (pl.ds(t * TILE, TILE), slice(None)),
        )
        for t in range(2)
    ]
    y_up[0].start()
    y_dn[1].start()
    start(k_win[:2])
    for copy in (y_up[1], y_dn[0], y_up[2], y_dn[3]):
        copy.start()
    start(k_win[2:3] + v_win[:3] + q_win[0][:3] + q_win[1][:3])

    def got(rsem, view, slot):
        copy = remote(view(OWN), view(slot), st_send.at[0, 0], rsem.at[slot], sibling)
        run(exists[slot - OWN], copy.wait_recv)

    def relay_when_far(rsem, view, relay):
        copy = remote(view(OWN), view(far_slot), st_send.at[0, 0], rsem.at[far_slot], sibling)

        @pl.when(relays)
        def _():
            copy.wait_recv()
            relay[0].start()

    def other_far(rsem, view):
        slot = 2 * SPAN - far_slot
        copy = remote(view(OWN), view(slot), st_send.at[0, 0], rsem.at[slot], sibling)
        run(from_relay, copy.wait_recv)

    def rest_of(rsem, view):
        other_far(rsem, view)
        got(rsem, view, 1)
        got(rsem, view, 3)

    def k_view(slot):
        return kwin.at[slot]

    def v_view(slot):
        return vwin.at[slot]

    def q_view(t):
        return lambda slot: qwin.at[slot, pl.ds(t * TILE, TILE)]

    def weight(slot):
        src = lax.rem(hd + (num_head - slot), num_head)
        return wv[:, pl.ds(pl.multiple_of(src * feat, 128), feat)]

    def tile_rows(t):
        return slice(t * TILE, (t + 1) * TILE)

    def cols_of(h):
        return slice(h * HEAD_DIM, (h + 1) * HEAD_DIM)

    def whole(win, h):
        return win[:, :, cols_of(h)].reshape(SLOTS * ROWS, HEAD_DIM)

    def half(win, h, t, slots):
        return jnp.concatenate([win[j, tile_rows(t), cols_of(h)] for j in slots], axis=0)

    local[0].wait()
    local[1].wait()
    acc[...] = dot_nt(gwin[0], weight(0))
    for copy in local[2:]:
        copy.wait()

    def live_bias(value, off):
        live = value > 0 if exists[off] is None else jnp.logical_and(value > 0, exists[off])
        return jnp.where(live, 0.0, NEG).astype(jnp.float32)

    q_bias = [
        [live_bias(mask_sm[col, 2 * pos + r], col // 2 - SPAN) for col in range(2 * SLOTS)] for r in range(2)
    ]

    y_up[0].wait_recv()
    y_fw[0].start()
    y_up[3].start()
    y_dn[1].wait_recv()
    y_fw[1].start()
    y_dn[2].start()

    relay_when_far(kvq_recv.at[0], k_view, k_win[3])
    rest_of(kvq_recv.at[0], k_view)

    lane = lax.broadcasted_iota(jnp.int32, (TILE, 128), 1)

    lse_cols = [jnp.zeros((TILE, 128), jnp.float32) for _ in range(2)]
    for h in range(heads):
        q_h = qwin[OWN, :, cols_of(h)]
        s = dot_nt(q_h, whole(kwin, h))
        for r in range(2):
            rows = tile_rows(r)
            top = None
            for col in range(2 * SLOTS):
                lanes = tile_rows(col)
                part = s[rows, lanes] * scale2 + q_bias[r][col]
                e_scr[h, rows, lanes] = part
                top = part if top is None else jnp.maximum(top, part)
            top = jnp.max(top, axis=1, keepdims=True)
            total = None
            for col in range(2 * SLOTS):
                lanes = tile_rows(col)
                e = jnp.exp2(e_scr[h, rows, lanes] - top)
                e_scr[h, rows, lanes] = e
                total = e if total is None else total + e
            total = jnp.sum(total, axis=1, keepdims=True)
            linv_scr[h, rows, :] = jnp.broadcast_to(1.0 / total, (TILE, 128))
            lse_cols[r] = jnp.where(lane == h, top + jnp.log2(total), lse_cols[r])
    for r in range(2):
        lse_win[OWN, :, tile_rows(r)] = jnp.transpose(lse_cols[r])[:STAT_ROWS, :]

    def stats(win, which, t):
        def view(slot):
            return win.at[slot, :, pl.ds(t * TILE, TILE)]

        return [
            (
                remote(view(OWN), view(OWN - off), st_send.at[which, i], st_recv.at[which, OWN - off], at_ctx(off)),
                exists[off],
            )
            for i, off in enumerate((-2, 2, -1, 1))
        ]

    lse_copies = stats(lse_win, 0, 0) + stats(lse_win, 1, 1)
    start(lse_copies)

    y_up[2].wait_recv()
    y_fw[2].start()
    y_dn[3].wait_recv()
    y_fw[3].start()

    lo, hi = tile_rows(0), tile_rows(1)
    y_up[1].wait_recv()
    y_dn[0].wait_recv()
    acc[lo] += dot_nt(gwin[1, lo], weight(1)) + dot_nt(gwin[3, lo], weight(3))

    relay_when_far(kvq_recv.at[1], v_view, v_win[3])

    y_fw[0].wait_recv()
    y_fw[1].wait_recv()
    dwin[OWN, lo] = (acc[lo] + dot_nt(gwin[2, lo], weight(2))).astype(jnp.bfloat16)
    rest_of(kvq_recv.at[1], v_view)

    for h in range(heads):
        out = dot_nn(e_scr[h].astype(jnp.bfloat16), whole(vwin, h))
        o_scr[:, cols_of(h)] = (out * linv_scr[h]).astype(jnp.bfloat16)

    lo_win = window(dwin.at[OWN, pl.ds(0, TILE)], dwin, lo_send, lo_recv, (pl.ds(0, TILE), slice(None)))
    start(lo_win[:3])

    def delta_of(t):
        rows = tile_rows(t)
        cols = jnp.zeros((TILE, 128), jnp.float32)
        for h in range(heads):
            delta = jnp.sum(
                dwin[OWN, rows, cols_of(h)].astype(jnp.float32) * o_scr[rows, cols_of(h)].astype(jnp.float32),
                axis=1,
                keepdims=True,
            )
            dcol_scr[h, rows] = jnp.broadcast_to(delta, (TILE, 128))
            cols = jnp.where(lane == h, delta, cols)
        del_win[OWN, :, rows] = jnp.transpose(cols)[:STAT_ROWS, :]

    def own_queries(t):
        rows = tile_rows(t)
        for h in range(heads):
            dp = dot_nt(dwin[OWN, rows, cols_of(h)], whole(vwin, h))
            delta = dcol_scr[h, rows]
            linv = linv_scr[h, rows]
            ds = [
                (e_scr[h, rows, tile_rows(col)] * linv * (dp[:, tile_rows(col)] - delta)).astype(jnp.bfloat16)
                for col in range(2 * SLOTS)
            ]
            out = dot_nn(jnp.concatenate(ds, axis=1), whole(kwin, h))
            dq_ref[rows, cols_of(h)] = (out * scale).astype(jnp.bfloat16)

    def slot_bias(j, t, r):
        block = lax.rem(pos + (j - SPAN + num_ctx), num_ctx)
        there = jnp.logical_and(pos + j >= SPAN, pos + j < num_ctx + SPAN)
        live = jnp.logical_and(mask_sm[r + 2 * (2 * SPAN - j), 2 * block + t] > 0, there)
        return jnp.full((1, TILE), jnp.where(live, 0.0, NEG), jnp.float32)

    def stat_row(win, h, t, slots):
        return jnp.concatenate([win[j, h : h + 1, tile_rows(t)] for j in slots], axis=1)

    def lanes_of(slots):
        return slice(0, 2 * TILE) if slots is early else slice(2 * TILE, SLOTS * TILE)

    def weights_t(t, slots):
        bias = [jnp.concatenate([slot_bias(j, t, r) for j in slots], axis=1) for r in range(2)]
        for h in range(heads):
            st = dot_nt(kwin[OWN, :, cols_of(h)], half(qwin, h, t, slots)) * scale2
            lse = stat_row(lse_win, h, t, slots)
            for r in range(2):
                pt_scr[h, t, tile_rows(r), lanes_of(slots)] = jnp.exp2(st[tile_rows(r)] - (lse - bias[r]))

    def own_keys(h, t, slots):
        d_t = half(dwin, h, t, slots)
        p = pt_scr[h, t, :, lanes_of(slots)]
        dv = dot_nn(p.astype(jnp.bfloat16), d_t)
        dp = dot_nt(vwin[OWN, :, cols_of(h)], d_t)
        ds = (p * (dp - stat_row(del_win, h, t, slots))).astype(jnp.bfloat16)
        return dot_nn(ds, half(qwin, h, t, slots)), dv

    def add_keys(h, t, slots, first=False):
        dk, dv = own_keys(h, t, slots)
        if first:
            dk_acc[:, cols_of(h)] = dk
            dv_acc[:, cols_of(h)] = dv
        else:
            dk_acc[:, cols_of(h)] += dk
            dv_acc[:, cols_of(h)] += dv

    def got_at(rsem, win, t, slot, cols=slice(None)):
        rows = pl.ds(t * TILE, TILE)
        remote(win.at[OWN, rows, cols], win.at[slot, rows, cols], st_send.at[0, 0], rsem.at[slot], sibling).wait_recv()

    def near_stats(win, which, t):
        lanes = pl.ds(t * TILE, TILE)
        remote(
            win.at[OWN, :, lanes],
            win.at[early[1], :, lanes],
            st_send.at[0, 0],
            st_recv.at[which, early[1]],
            sibling,
        ).wait_recv()

    def far_stats(win, which, t):
        view = lambda slot: win.at[slot, :, pl.ds(t * TILE, TILE)]
        for slot in (0, 4):
            got(st_recv.at[which], view, slot)
        copy = remote(view(OWN), view(late[2]), st_send.at[0, 0], st_recv.at[which, late[2]], sibling)
        run(from_relay, copy.wait_recv)

    def relayed(rsem, view):
        other_far(rsem, view)
        copy = remote(view(OWN), view(late[2]), st_send.at[0, 0], rsem.at[late[2]], sibling)
        run(from_relay, copy.wait_recv)

    delta_of(0)
    del_copies = stats(del_win, 2, 0)
    start(del_copies)
    own_queries(0)

    got_at(kvq_recv.at[2], qwin, 0, early[1])
    got_at(kvq_recv.at[3], qwin, 1, early[1])
    near_stats(lse_win, 0, 0)
    near_stats(lse_win, 1, 1)
    weights_t(0, early)
    weights_t(1, early)
    relay_when_far(kvq_recv.at[2], q_view(0), q_win[0][3])
    y_up[3].wait_recv()
    y_dn[2].wait_recv()
    acc[hi] += dot_nt(gwin[1, hi], weight(1)) + dot_nt(gwin[3, hi], weight(3))
    got_at(lo_recv, dwin, 0, early[1])
    near_stats(del_win, 2, 0)
    for h in range(heads):
        add_keys(h, 0, early, first=True)

    relayed(kvq_recv.at[2], q_view(0))
    far_stats(lse_win, 0, 0)
    far_stats(lse_win, 1, 1)
    weights_t(0, late)
    relay_when_far(kvq_recv.at[3], q_view(1), q_win[1][3])

    y_fw[2].wait_recv()
    y_fw[3].wait_recv()
    dwin[OWN, hi] = (acc[hi] + dot_nt(gwin[2, hi], weight(2))).astype(jnp.bfloat16)
    delta_of(1)
    hi_copies = stats(del_win, 3, 1)

    groups = GROUPS

    def hi_part(g):
        first, last = groups[g]
        return pl.ds(TILE, TILE), pl.ds(first * HEAD_DIM, (last - first) * HEAD_DIM)

    def hi_view(g):
        return lambda slot: dwin.at[slot, hi_part(g)[0], hi_part(g)[1]]

    hi_win = [
        window(hi_view(g)(OWN), dwin, d_send.at[g], d_recv.at[g], hi_part(g)) for g in range(len(groups))
    ]
    start(hi_win[0][:3] + tuple(hi_copies))
    for items in hi_win[1:]:
        start(items[:3])

    def hi_relay(g):
        relay_when_far(d_recv.at[g], hi_view(g), hi_win[g][3])

    relayed(kvq_recv.at[3], q_view(1))
    weights_t(1, late)
    own_queries(1)

    def lo_view(slot):
        return dwin.at[slot, pl.ds(0, TILE)]

    relay_when_far(lo_recv, lo_view, lo_win[3])
    near_stats(del_win, 3, 1)
    for g, (first, last) in enumerate(groups):
        got_at(d_recv.at[g], dwin, 1, early[1], hi_part(g)[1])
        for h in range(first, last):
            add_keys(h, 1, early)
    relayed(lo_recv, lo_view)
    far_stats(del_win, 2, 0)
    for h in range(heads):
        add_keys(h, 0, late)
        if h == 2:
            hi_relay(0)
    far_stats(del_win, 3, 1)

    def finish(h):
        dk, dv = own_keys(h, 1, late)
        dv_ref[:, cols_of(h)] = (dv_acc[:, cols_of(h)] + dv).astype(jnp.bfloat16)
        dk_ref[:, cols_of(h)] = ((dk_acc[:, cols_of(h)] + dk) * scale).astype(jnp.bfloat16)

    for g, (first, last) in enumerate(groups):
        if g == 0:
            hi_relay(1)
        relayed(d_recv.at[g], hi_view(g))
        for h in range(first, last):
            finish(h)

    for copy in y_up + y_dn + y_fw:
        copy.wait_send()
    for items in [k_win, v_win, *q_win, lo_win, lse_copies, del_copies, hi_copies, *hi_win]:
        for copy, cond in items:
            run(cond, copy.wait_send)


def write_out(a_ref, b_ref, c_ref, a_out, b_out, c_out, sems):
    copies = [
        pltpu.make_async_copy(src, dst, sems.at[i])
        for i, (src, dst) in enumerate(((a_ref, a_out), (b_ref, b_out), (c_ref, c_out)))
    ]
    for copy in copies:
        copy.start()
    for copy in copies:
        copy.wait()


def local(num_ctx, num_head, queries, keys, values, out_weight, reward_grad, tile_mask):
    rows, width = queries.shape
    feat = reward_grad.shape[1]
    heads = width // HEAD_DIM
    mask_cols = tile_mask.T
    out = jax.ShapeDtypeStruct((rows, width), jnp.bfloat16)
    win = pltpu.VMEM((SLOTS, rows, width), jnp.bfloat16)
    stat = pltpu.VMEM((SLOTS, STAT_ROWS, rows), jnp.float32)
    col = pltpu.VMEM((heads, rows, 128), jnp.float32)
    full = pltpu.VMEM((rows, width), jnp.float32)
    dma = pltpu.SemaphoreType.DMA
    grads = pl.pallas_call(
        functools.partial(kernel, num_ctx, num_head),
        out_shape=(pltpu.VMEM((rows, width), jnp.bfloat16),) * 3,
        in_specs=[pl.BlockSpec(memory_space=pltpu.HBM)] * 6,
        out_specs=[pl.BlockSpec(memory_space=pltpu.VMEM)] * 3,
        scratch_shapes=[
            win,
            win,
            win,
            win,
            pltpu.VMEM((num_head, rows, feat), jnp.bfloat16),
            pltpu.VMEM(out_weight.shape, jnp.bfloat16),
            pltpu.SMEM(mask_cols.shape, jnp.int32),
            full,
            pltpu.VMEM((heads, rows, SLOTS * rows), jnp.float32),
            pltpu.VMEM((heads, 2, rows, SLOTS * TILE), jnp.float32),
            pltpu.VMEM((rows, width), jnp.bfloat16),
            col,
            col,
            full,
            full,
            stat,
            stat,
            dma((6,)),
            dma((4, 4)),
            dma((4, SLOTS)),
            dma((12,)),
            dma((12,)),
            dma((4,)),
            dma((SLOTS,)),
            dma((heads, 4)),
            dma((heads, SLOTS)),
            dma((4, 4)),
            dma((4, SLOTS)),
        ],
        compiler_params=pltpu.CompilerParams(
            collective_id=0, has_side_effects=True, vmem_limit_bytes=VMEM_MB * 1024 * 1024
        ),
        name="halo_attention_backward",
    )(*[pltpu.with_memory_space_constraint(x, pltpu.HBM) for x in (queries, keys, values, out_weight, reward_grad, mask_cols)])
    return pl.pallas_call(
        write_out,
        out_shape=(out, out, out),
        in_specs=[pl.BlockSpec(memory_space=pltpu.VMEM)] * 3,
        out_specs=[pl.BlockSpec(memory_space=pltpu.HBM)] * 3,
        scratch_shapes=[dma((3,))],
        compiler_params=pltpu.CompilerParams(vmem_limit_bytes=262144),
        name="write_out",
    )(*grads)


def solution(mesh):
    placed = (
        P("ctx", "head"),
        P("ctx", "head"),
        P("ctx", "head"),
        P("head", None),
        P("ctx", "head"),
        P(),
    )
    return jax.shard_map(
        functools.partial(local, mesh.shape["ctx"], mesh.shape["head"]),
        mesh=mesh,
        in_specs=placed,
        out_specs=(P("ctx", "head"), P("ctx", "head"), P("ctx", "head")),
        check_vma=False,
    )
```

```python
import functools
import math

import jax
import jax.numpy as jnp
from jax import lax
from jax.experimental import pallas as pl
from jax.experimental.pallas import tpu as pltpu
from jax.sharding import PartitionSpec as P

HEAD_DIM = 128
TILE = 128
SPAN = 2
SLOTS = 2 * SPAN + 1
OWN = SPAN
ROWS = 2 * TILE
STAT_ROWS = 8
NEG = -1.0e30
LOG2E = 1.4426950408889634
VMEM_MB = 60
GROUPS = ((0, 3), (3, 5))
MESH = pl.DeviceIdType.MESH


def dot_nt(a, b):
    return lax.dot_general(a, b, (((1,), (1,)), ((), ())), preferred_element_type=jnp.float32)


def dot_nn(a, b):
    return lax.dot_general(a, b, (((1,), (0,)), ((), ())), preferred_element_type=jnp.float32)


def kernel(
    num_ctx,
    num_head,
    q_hbm,
    k_hbm,
    v_hbm,
    w_hbm,
    g_hbm,
    mask_hbm,
    dq_ref,
    dk_ref,
    dv_ref,
    kwin,
    vwin,
    qwin,
    dwin,
    gwin,
    wv,
    mask_sm,
    acc,
    e_scr,
    pt_scr,
    o_scr,
    linv_scr,
    dcol_scr,
    dk_acc,
    dv_acc,
    lse_win,
    del_win,
    loc_sem,
    kvq_send,
    kvq_recv,
    y_send,
    y_recv,
    lo_send,
    lo_recv,
    d_send,
    d_recv,
    st_send,
    st_recv,
):
    heads = q_hbm.shape[1] // HEAD_DIM
    feat = g_hbm.shape[1]
    pos = lax.axis_index("ctx")
    hd = lax.axis_index("head")
    par = lax.rem(pos, 2)
    scale = 1.0 / math.sqrt(HEAD_DIM)
    scale2 = scale * LOG2E

    def at_ctx(off):
        return (lax.rem(pos + (off + num_ctx), num_ctx), hd)

    def at_head(off):
        return (pos, lax.rem(hd + (off + num_head), num_head))

    sibling = (pos + 1 - 2 * par, hd)

    exists = {
        off: None if off == 0 else (pos >= -off if off < 0 else pos < num_ctx - off) for off in range(-SPAN, SPAN + 1)
    }
    from_relay = jnp.where(par == 0, pos, num_ctx - 1 - pos) > 0
    relays = jnp.where(par == 0, pos + SPAN, num_ctx + 1 - pos) < num_ctx

    def run(cond, action):
        if cond is None:
            action()
        else:
            pl.when(cond)(action)

    def start(items):
        for copy, cond in items:
            run(cond, copy.start)

    local = [
        pltpu.make_async_copy(g_hbm, gwin.at[0], loc_sem.at[0]),
        pltpu.make_async_copy(w_hbm, wv, loc_sem.at[1]),
        pltpu.make_async_copy(q_hbm, qwin.at[OWN], loc_sem.at[2]),
        pltpu.make_async_copy(k_hbm, kwin.at[OWN], loc_sem.at[3]),
        pltpu.make_async_copy(v_hbm, vwin.at[OWN], loc_sem.at[4]),
        pltpu.make_async_copy(mask_hbm, mask_sm, loc_sem.at[5]),
    ]

    barrier = pltpu.get_barrier_semaphore()


    def greet(who):
        return lambda: pl.semaphore_signal(barrier, inc=1, device_id=who, device_id_type=MESH)

    arrivals = 2
    for off in (-2, 2, -1, 1):
        run(exists[off], greet(at_ctx(off)))
        arrivals = arrivals + exists[off].astype(jnp.int32)
    greet(at_head(1))()
    greet(at_head(-1))()
    for copy in local:
        copy.start()
    for off in (-2, 2, -1, 1):

        @pl.when(jnp.logical_not(exists[off]))
        def _():
            for win in (kwin, vwin, qwin, dwin, lse_win, del_win):
                win[OWN + off] = jnp.zeros(win.shape[1:], win.dtype)

    pl.semaphore_wait(barrier, arrivals)

    def remote(src, dst, ssem, rsem, who):
        return pltpu.make_async_remote_copy(
            src_ref=src, dst_ref=dst, send_sem=ssem, recv_sem=rsem, device_id=who, device_id_type=MESH
        )

    up, down = at_head(1), at_head(-1)

    def quarter(n):
        return pl.ds(n * (ROWS // 4), ROWS // 4)

    y_up = [remote(g_hbm.at[quarter(n)], gwin.at[1, quarter(n)], y_send.at[n], y_recv.at[n], up) for n in range(4)]
    y_dn = [
        remote(g_hbm.at[quarter(n)], gwin.at[3, quarter(n)], y_send.at[4 + n], y_recv.at[4 + n], down)
        for n in range(4)
    ]
    y_fw = [
        remote(
            gwin.at[3 if n % 2 else 1, quarter(n)],
            gwin.at[2, quarter(n)],
            y_send.at[8 + n],
            y_recv.at[8 + n],
            down if n % 2 else up,
        )
        for n in range(4)
    ]

    far_slot = 2 * SPAN - 2 * SPAN * par
    relay_dst = 3 - 2 * par
    ahead = 4 * par - 2
    relays_back = jnp.logical_and(pos - ahead >= 0, pos - ahead < num_ctx)
    relays_on = jnp.logical_and(pos + ahead >= 0, pos + ahead < num_ctx)
    near_dst = 1 + 2 * par
    early, late = (OWN, 3 - 2 * par), (0, 2 * SPAN, 1 + 2 * par)

    def window(src, win, ssem, rsem, part=None):
        def view(ref):
            return ref if part is None else ref.at[part[0], part[1]]

        relay_src, relay_to = view(win.at[far_slot]), view(win.at[relay_dst])
        return (
            (remote(src, view(win.at[4 * (1 - par)]), ssem.at[0], rsem.at[4 * (1 - par)], at_ctx(ahead)), relays_on),
            (remote(src, view(win.at[4 * par]), ssem.at[1], rsem.at[4 * par], at_ctx(-ahead)), relays_back),
            (remote(src, view(win.at[near_dst]), ssem.at[2], rsem.at[near_dst], sibling), None),
            (remote(relay_src, relay_to, ssem.at[3], rsem.at[relay_dst], sibling), relays),
        )

    k_win = window(k_hbm, kwin, kvq_send.at[0], kvq_recv.at[0])
    v_win = window(v_hbm, vwin, kvq_send.at[1], kvq_recv.at[1])
    q_win = [
        window(
            q_hbm.at[pl.ds(t * TILE, TILE)],
            qwin,
            kvq_send.at[2 + t],
            kvq_recv.at[2 + t],
            (pl.ds(t * TILE, TILE), slice(None)),
        )
        for t in range(2)
    ]
    y_up[0].start()
    y_dn[1].start()
    start(k_win[:2])
    for copy in (y_up[1], y_dn[0], y_up[2], y_dn[3]):
        copy.start()
    start(k_win[2:3] + v_win[:3] + q_win[0][:3] + q_win[1][:3])

    def got(rsem, view, slot):
        copy = remote(view(OWN), view(slot), st_send.at[0, 0], rsem.at[slot], sibling)
        run(exists[slot - OWN], copy.wait_recv)

    def relay_when_far(rsem, view, relay):
        copy = remote(view(OWN), view(far_slot), st_send.at[0, 0], rsem.at[far_slot], sibling)

        @pl.when(relays)
        def _():
            copy.wait_recv()
            relay[0].start()

    def other_far(rsem, view):
        slot = 2 * SPAN - far_slot
        copy = remote(view(OWN), view(slot), st_send.at[0, 0], rsem.at[slot], sibling)
        run(from_relay, copy.wait_recv)

    def rest_of(rsem, view):
        other_far(rsem, view)
        got(rsem, view, 1)
        got(rsem, view, 3)

    def k_view(slot):
        return kwin.at[slot]

    def v_view(slot):
        return vwin.at[slot]

    def q_view(t):
        return lambda slot: qwin.at[slot, pl.ds(t * TILE, TILE)]

    def weight(slot):
        src = lax.rem(hd + (num_head - slot), num_head)
        return wv[:, pl.ds(pl.multiple_of(src * feat, 128), feat)]

    def tile_rows(t):
        return slice(t * TILE, (t + 1) * TILE)

    def cols_of(h):
        return slice(h * HEAD_DIM, (h + 1) * HEAD_DIM)

    def whole(win, h):
        return win[:, :, cols_of(h)].reshape(SLOTS * ROWS, HEAD_DIM)

    def half(win, h, t, slots):
        return jnp.concatenate([win[j, tile_rows(t), cols_of(h)] for j in slots], axis=0)

    local[0].wait()
    local[1].wait()
    acc[...] = dot_nt(gwin[0], weight(0))
    for copy in local[2:]:
        copy.wait()

    def live_bias(value, off):
        live = value > 0 if exists[off] is None else jnp.logical_and(value > 0, exists[off])
        return jnp.where(live, 0.0, NEG).astype(jnp.float32)

    q_bias = [
        [live_bias(mask_sm[col, 2 * pos + r], col // 2 - SPAN) for col in range(2 * SLOTS)] for r in range(2)
    ]

    y_up[0].wait_recv()
    y_fw[0].start()
    y_up[3].start()
    y_dn[1].wait_recv()
    y_fw[1].start()
    y_dn[2].start()

    relay_when_far(kvq_recv.at[0], k_view, k_win[3])
    rest_of(kvq_recv.at[0], k_view)

    lane = lax.broadcasted_iota(jnp.int32, (TILE, 128), 1)

    lse_cols = [jnp.zeros((TILE, 128), jnp.float32) for _ in range(2)]
    for h in range(heads):
        q_h = qwin[OWN, :, cols_of(h)]
        s = dot_nt(q_h, whole(kwin, h))
        for r in range(2):
            rows = tile_rows(r)
            top = None
            for col in range(2 * SLOTS):
                lanes = tile_rows(col)
                part = s[rows, lanes] * scale2 + q_bias[r][col]
                e_scr[h, rows, lanes] = part
                top = part if top is None else jnp.maximum(top, part)
            top = jnp.max(top, axis=1, keepdims=True)
            total = None
            for col in range(2 * SLOTS):
                lanes = tile_rows(col)
                e = jnp.exp2(e_scr[h, rows, lanes] - top)
                e_scr[h, rows, lanes] = e
                total = e if total is None else total + e
            total = jnp.sum(total, axis=1, keepdims=True)
            linv_scr[h, rows, :] = jnp.broadcast_to(1.0 / total, (TILE, 128))
            lse_cols[r] = jnp.where(lane == h, top + jnp.log2(total), lse_cols[r])
    for r in range(2):
        lse_win[OWN, :, tile_rows(r)] = jnp.transpose(lse_cols[r])[:STAT_ROWS, :]

    def stats(win, which, t):
        def view(slot):
            return win.at[slot, :, pl.ds(t * TILE, TILE)]

        return [
            (
                remote(view(OWN), view(OWN - off), st_send.at[which, i], st_recv.at[which, OWN - off], at_ctx(off)),
                exists[off],
            )
            for i, off in enumerate((-2, 2, -1, 1))
        ]

    lse_copies = stats(lse_win, 0, 0) + stats(lse_win, 1, 1)
    start(lse_copies)

    y_up[2].wait_recv()
    y_fw[2].start()
    y_dn[3].wait_recv()
    y_fw[3].start()

    lo, hi = tile_rows(0), tile_rows(1)
    y_up[1].wait_recv()
    y_dn[0].wait_recv()
    acc[lo] += dot_nt(gwin[1, lo], weight(1)) + dot_nt(gwin[3, lo], weight(3))

    relay_when_far(kvq_recv.at[1], v_view, v_win[3])

    y_fw[0].wait_recv()
    y_fw[1].wait_recv()
    dwin[OWN, lo] = (acc[lo] + dot_nt(gwin[2, lo], weight(2))).astype(jnp.bfloat16)
    rest_of(kvq_recv.at[1], v_view)

    for h in range(heads):
        out = dot_nn(e_scr[h].astype(jnp.bfloat16), whole(vwin, h))
        o_scr[:, cols_of(h)] = (out * linv_scr[h]).astype(jnp.bfloat16)

    lo_win = window(dwin.at[OWN, pl.ds(0, TILE)], dwin, lo_send, lo_recv, (pl.ds(0, TILE), slice(None)))
    start(lo_win[:3])

    def delta_of(t):
        rows = tile_rows(t)
        cols = jnp.zeros((TILE, 128), jnp.float32)
        for h in range(heads):
            delta = jnp.sum(
                dwin[OWN, rows, cols_of(h)].astype(jnp.float32) * o_scr[rows, cols_of(h)].astype(jnp.float32),
                axis=1,
                keepdims=True,
            )
            dcol_scr[h, rows] = jnp.broadcast_to(delta, (TILE, 128))
            cols = jnp.where(lane == h, delta, cols)
        del_win[OWN, :, rows] = jnp.transpose(cols)[:STAT_ROWS, :]

    def own_queries(t):
        rows = tile_rows(t)
        for h in range(heads):
            dp = dot_nt(dwin[OWN, rows, cols_of(h)], whole(vwin, h))
            delta = dcol_scr[h, rows]
            linv = linv_scr[h, rows]
            ds = [
                (e_scr[h, rows, tile_rows(col)] * linv * (dp[:, tile_rows(col)] - delta)).astype(jnp.bfloat16)
                for col in range(2 * SLOTS)
            ]
            out = dot_nn(jnp.concatenate(ds, axis=1), whole(kwin, h))
            dq_ref[rows, cols_of(h)] = (out * scale).astype(jnp.bfloat16)

    def slot_bias(j, t, r):
        block = lax.rem(pos + (j - SPAN + num_ctx), num_ctx)
        there = jnp.logical_and(pos + j >= SPAN, pos + j < num_ctx + SPAN)
        live = jnp.logical_and(mask_sm[r + 2 * (2 * SPAN - j), 2 * block + t] > 0, there)
        return jnp.full((1, TILE), jnp.where(live, 0.0, NEG), jnp.float32)

    def stat_row(win, h, t, slots):
        return jnp.concatenate([win[j, h : h + 1, tile_rows(t)] for j in slots], axis=1)

    def lanes_of(slots):
        return slice(0, 2 * TILE) if slots is early else slice(2 * TILE, SLOTS * TILE)

    def weights_t(t, slots):
        bias = [jnp.concatenate([slot_bias(j, t, r) for j in slots], axis=1) for r in range(2)]
        for h in range(heads):
            st = dot_nt(kwin[OWN, :, cols_of(h)], half(qwin, h, t, slots)) * scale2
            lse = stat_row(lse_win, h, t, slots)
            for r in range(2):
                pt_scr[h, t, tile_rows(r), lanes_of(slots)] = jnp.exp2(st[tile_rows(r)] - (lse - bias[r]))

    def own_keys(h, t, slots):
        d_t = half(dwin, h, t, slots)
        p = pt_scr[h, t, :, lanes_of(slots)]
        dv = dot_nn(p.astype(jnp.bfloat16), d_t)
        dp = dot_nt(vwin[OWN, :, cols_of(h)], d_t)
        ds = (p * (dp - stat_row(del_win, h, t, slots))).astype(jnp.bfloat16)
        return dot_nn(ds, half(qwin, h, t, slots)), dv

    def add_keys(h, t, slots, first=False):
        dk, dv = own_keys(h, t, slots)
        if first:
            dk_acc[:, cols_of(h)] = dk
            dv_acc[:, cols_of(h)] = dv
        else:
            dk_acc[:, cols_of(h)] += dk
            dv_acc[:, cols_of(h)] += dv

    def got_at(rsem, win, t, slot, cols=slice(None)):
        rows = pl.ds(t * TILE, TILE)
        remote(win.at[OWN, rows, cols], win.at[slot, rows, cols], st_send.at[0, 0], rsem.at[slot], sibling).wait_recv()

    def near_stats(win, which, t):
        lanes = pl.ds(t * TILE, TILE)
        remote(
            win.at[OWN, :, lanes],
            win.at[early[1], :, lanes],
            st_send.at[0, 0],
            st_recv.at[which, early[1]],
            sibling,
        ).wait_recv()

    def far_stats(win, which, t):
        view = lambda slot: win.at[slot, :, pl.ds(t * TILE, TILE)]
        for slot in (0, 4):
            got(st_recv.at[which], view, slot)
        copy = remote(view(OWN), view(late[2]), st_send.at[0, 0], st_recv.at[which, late[2]], sibling)
        run(from_relay, copy.wait_recv)

    def relayed(rsem, view):
        other_far(rsem, view)
        copy = remote(view(OWN), view(late[2]), st_send.at[0, 0], rsem.at[late[2]], sibling)
        run(from_relay, copy.wait_recv)

    delta_of(0)
    del_copies = stats(del_win, 2, 0)
    start(del_copies)
    own_queries(0)

    got_at(kvq_recv.at[2], qwin, 0, early[1])
    got_at(kvq_recv.at[3], qwin, 1, early[1])
    near_stats(lse_win, 0, 0)
    near_stats(lse_win, 1, 1)
    weights_t(0, early)
    weights_t(1, early)
    relay_when_far(kvq_recv.at[2], q_view(0), q_win[0][3])
    y_up[3].wait_recv()
    y_dn[2].wait_recv()
    acc[hi] += dot_nt(gwin[1, hi], weight(1)) + dot_nt(gwin[3, hi], weight(3))
    got_at(lo_recv, dwin, 0, early[1])
    near_stats(del_win, 2, 0)
    for h in range(heads):
        add_keys(h, 0, early, first=True)

    relayed(kvq_recv.at[2], q_view(0))
    far_stats(lse_win, 0, 0)
    far_stats(lse_win, 1, 1)
    weights_t(0, late)
    relay_when_far(kvq_recv.at[3], q_view(1), q_win[1][3])

    y_fw[2].wait_recv()
    y_fw[3].wait_recv()
    dwin[OWN, hi] = (acc[hi] + dot_nt(gwin[2, hi], weight(2))).astype(jnp.bfloat16)
    delta_of(1)
    hi_copies = stats(del_win, 3, 1)

    groups = GROUPS

    def hi_part(g):
        first, last = groups[g]
        return pl.ds(TILE, TILE), pl.ds(first * HEAD_DIM, (last - first) * HEAD_DIM)

    def hi_view(g):
        return lambda slot: dwin.at[slot, hi_part(g)[0], hi_part(g)[1]]

    hi_win = [
        window(hi_view(g)(OWN), dwin, d_send.at[g], d_recv.at[g], hi_part(g)) for g in range(len(groups))
    ]
    start(hi_win[0][:3] + tuple(hi_copies))
    for items in hi_win[1:]:
        start(items[:3])

    def hi_relay(g):
        relay_when_far(d_recv.at[g], hi_view(g), hi_win[g][3])

    relayed(kvq_recv.at[3], q_view(1))
    weights_t(1, late)
    own_queries(1)

    def lo_view(slot):
        return dwin.at[slot, pl.ds(0, TILE)]

    relay_when_far(lo_recv, lo_view, lo_win[3])
    near_stats(del_win, 3, 1)
    for g, (first, last) in enumerate(groups):
        got_at(d_recv.at[g], dwin, 1, early[1], hi_part(g)[1])
        for h in range(first, last):
            add_keys(h, 1, early)
    relayed(lo_recv, lo_view)
    far_stats(del_win, 2, 0)
    for h in range(heads):
        add_keys(h, 0, late)
        if h == 2:
            hi_relay(0)
    far_stats(del_win, 3, 1)

    def finish(h):
        dk, dv = own_keys(h, 1, late)
        dv_ref[:, cols_of(h)] = (dv_acc[:, cols_of(h)] + dv).astype(jnp.bfloat16)
        dk_ref[:, cols_of(h)] = ((dk_acc[:, cols_of(h)] + dk) * scale).astype(jnp.bfloat16)

    for g, (first, last) in enumerate(groups):
        relayed(d_recv.at[g], hi_view(g))
        for h in range(first, last):
            finish(h)
            if h == 0:
                hi_relay(1)

    for copy in y_up + y_dn + y_fw:
        copy.wait_send()
    for items in [k_win, v_win, *q_win, lo_win, lse_copies, del_copies, hi_copies, *hi_win]:
        for copy, cond in items:
            run(cond, copy.wait_send)


def write_out(a_ref, b_ref, c_ref, a_out, b_out, c_out, sems):
    copies = [
        pltpu.make_async_copy(src, dst, sems.at[i])
        for i, (src, dst) in enumerate(((a_ref, a_out), (b_ref, b_out), (c_ref, c_out)))
    ]
    for copy in copies:
        copy.start()
    for copy in copies:
        copy.wait()


def local(num_ctx, num_head, queries, keys, values, out_weight, reward_grad, tile_mask):
    rows, width = queries.shape
    feat = reward_grad.shape[1]
    heads = width // HEAD_DIM
    mask_cols = tile_mask.T
    out = jax.ShapeDtypeStruct((rows, width), jnp.bfloat16)
    win = pltpu.VMEM((SLOTS, rows, width), jnp.bfloat16)
    stat = pltpu.VMEM((SLOTS, STAT_ROWS, rows), jnp.float32)
    col = pltpu.VMEM((heads, rows, 128), jnp.float32)
    full = pltpu.VMEM((rows, width), jnp.float32)
    dma = pltpu.SemaphoreType.DMA
    grads = pl.pallas_call(
        functools.partial(kernel, num_ctx, num_head),
        out_shape=(pltpu.VMEM((rows, width), jnp.bfloat16),) * 3,
        in_specs=[pl.BlockSpec(memory_space=pltpu.HBM)] * 6,
        out_specs=[pl.BlockSpec(memory_space=pltpu.VMEM)] * 3,
        scratch_shapes=[
            win,
            win,
            win,
            win,
            pltpu.VMEM((num_head, rows, feat), jnp.bfloat16),
            pltpu.VMEM(out_weight.shape, jnp.bfloat16),
            pltpu.SMEM(mask_cols.shape, jnp.int32),
            full,
            pltpu.VMEM((heads, rows, SLOTS * rows), jnp.float32),
            pltpu.VMEM((heads, 2, rows, SLOTS * TILE), jnp.float32),
            pltpu.VMEM((rows, width), jnp.bfloat16),
            col,
            col,
            full,
            full,
            stat,
            stat,
            dma((6,)),
            dma((4, 4)),
            dma((4, SLOTS)),
            dma((12,)),
            dma((12,)),
            dma((4,)),
            dma((SLOTS,)),
            dma((heads, 4)),
            dma((heads, SLOTS)),
            dma((4, 4)),
            dma((4, SLOTS)),
        ],
        compiler_params=pltpu.CompilerParams(
            collective_id=0, has_side_effects=True, vmem_limit_bytes=VMEM_MB * 1024 * 1024
        ),
        name="halo_attention_backward",
    )(*[pltpu.with_memory_space_constraint(x, pltpu.HBM) for x in (queries, keys, values, out_weight, reward_grad, mask_cols)])
    return pl.pallas_call(
        write_out,
        out_shape=(out, out, out),
        in_specs=[pl.BlockSpec(memory_space=pltpu.VMEM)] * 3,
        out_specs=[pl.BlockSpec(memory_space=pltpu.HBM)] * 3,
        scratch_shapes=[dma((3,))],
        compiler_params=pltpu.CompilerParams(vmem_limit_bytes=262144),
        name="write_out",
    )(*grads)


def solution(mesh):
    placed = (
        P("ctx", "head"),
        P("ctx", "head"),
        P("ctx", "head"),
        P("head", None),
        P("ctx", "head"),
        P(),
    )
    return jax.shard_map(
        functools.partial(local, mesh.shape["ctx"], mesh.shape["head"]),
        mesh=mesh,
        in_specs=placed,
        out_specs=(P("ctx", "head"), P("ctx", "head"), P("ctx", "head")),
        check_vma=False,
    )
```
